32 devices in a mesh: groups: 2 (over y), tgt: 4 (over z), src: 2 (over x), sub: 2 (over core).
Axes of the slice: x: 2, y: 2, z: 4, core: 2. Of those that a mesh axis runs over, the one named last changes fastest.
Arguments:
- positions: float32 [3, 8192], P(None, ('groups', 'tgt', 'src', 'sub')), parts along dimension 1, may hold values from 0 to 40
- forces: float32 [3, 8192], P(None, ('groups', 'tgt', 'src', 'sub')), parts along dimension 1, may hold values from -0.6 to 0.6
- membership: int32 [8192], P(('groups', 'tgt', 'src', 'sub')), parts along dimension 0, may hold values from 0 to 15, never falling along the last dimension, each value on 1 to 1024 neighbouring positions
- owner_slot: int32 [32], P('groups'), parts along dimension 0, may hold values from 0 to 15, each once
Outputs:
- velocity: float32 [3, 8192], P(None, ('groups', 'tgt', 'src', 'sub')), parts along dimension 1
- rigid: float32 [9, 32], P(None, ('groups', 'tgt', 'src', 'sub')), parts along dimension 1
The draws below stay inside these ranges and needn't reach their ends.
There are 2 independent parts, one for each index of `groups`. The reference program is written for one: setup_inputs(seed, part) draws one part's arguments, and reference() takes and returns one part's arrays. A program takes and returns all parts, laid end to end along the dimension named above; each array names one. Nothing has to cross between parts.
Inputs may be any that keep to these rules, and one draw needn't show every extreme that they name: `membership`: monomers of one aggregate are consecutive; every aggregate holds 1 to 1024 monomers and one holds exactly 1024. `owner_slot`: a permutation; aggregate a's results go to column owner_slot[a] of rigid.
All inputs are finite; a program needn't handle non-finite values.
Results may differ from the reference program's by a relative error of at most 0.0003.
Values sent between devices are 32-bit elements; how exact they have to be, the bound alone decides.
No kernel may reach another device: no remote copies, remote signals or barrier semaphores. Data moves between devices by JAX's collectives and lax.ppermute only.
A program may use at most 64 MiB of HBM per device.

```python
import math
import jax
import jax.numpy as jnp
import numpy as np
from jax import lax

MOST = 1024
MONOMERS = 4096
AGG = 16


def shard_levels(own_key, shape, cuts, smallest, high):
    def one(position, shards_of):
        steps = jax.random.uniform(jax.random.fold_in(jax.random.fold_in(own_key, 6), position), (shards_of,), jnp.float32, smallest / len(cuts), high / len(cuts))
        return jnp.repeat(jnp.exp(steps), shape[position] // shards_of).reshape((-1,) + (1,) * (len(shape) - position - 1))

    level = one(*cuts[0])
    for cut in cuts[1:]:
        level = level * one(*cut)
    return level


def length_profile(count, total, bound, skew):
    loads = [(1 << 20) // math.isqrt(standing ** skew) + 1 for standing in range(2, count + 1)]
    surplus, given = total - bound - (count - 1), [1] * (count - 1)
    while surplus > 0:
        candidates = [i for i in range(count - 1) if given[i] < bound]
        mass, remaining = sum([loads[i] for i in candidates]), surplus
        for i in candidates:
            more = min(bound - given[i], max(1, remaining * loads[i] // mass), surplus)
            given[i] = given[i] + more
            surplus = surplus - more
    return np.array([bound] + given)


def ragged(key, number_of, total, reach, skew):
    if number_of == 2:
        one = jax.random.randint(key, (), max(1, total - reach), min(reach, total - 1) + 1)
        return jnp.stack([one, total - one])
    tallies = jnp.asarray(length_profile(number_of, total, reach, skew), jnp.int32)
    twos = (number_of - 1) // 2
    donor, receiver = tallies[1:1 + 2 * twos:2], tallies[2:2 + 2 * twos:2]
    margin = jnp.minimum(donor - 1, reach - receiver)
    shifted = jax.random.randint(jax.random.fold_in(key, 1), (twos,), 0, 1 << 20) % (margin + 1)
    tallies = tallies.at[1:1 + 2 * twos:2].set(donor - shifted).at[2:2 + 2 * twos:2].set(receiver + shifted)
    return tallies[jax.random.permutation(jax.random.fold_in(key, 2), number_of)]


def normal_values(key, shape, spread, bound, shards=(), held_as=jnp.bfloat16):
    loudness = shard_levels(key, shape, shards, -0.22, 0.18) if shards else 1.0
    values = jax.random.normal(key, shape, jnp.float32) * spread * loudness
    return jnp.minimum(jnp.maximum(values, -bound), bound).astype(held_as)


def setup_inputs(seed: int = 0, part: int = 0) -> dict:
    streams_of = jax.random.split(jax.random.key(seed), 5)
    own_keys = jax.random.split(jax.random.fold_in(streams_of[4], part), 5)
    return {
        "positions": jnp.clip(40.0 * jax.random.uniform(own_keys[0], (3, MONOMERS), jnp.float32) ** shard_levels(own_keys[0], (3, MONOMERS), ((1, 16),), -0.2, 0.2), 0.0, 40.0),
        "forces": normal_values(own_keys[1], (3, MONOMERS), 0.1, 0.6, ((1, 16),), jnp.float32),
        "membership": jnp.searchsorted(jnp.cumsum(ragged(own_keys[2], AGG, MONOMERS, MOST, 2)), jnp.arange(MONOMERS), side="right").astype(jnp.int32),
        "owner_slot": jax.random.permutation(own_keys[3], AGG).astype(jnp.int32),
    }


radius = 1.0

def pair_sum(target_pos, source_pos, source_force):
    offset = target_pos[:, :, None] - source_pos[:, None, :]
    dist_sq = lax.optimization_barrier(jnp.sum(offset * offset, axis=0))
    nonzero = dist_sq > 0.0
    inverse = jnp.where(nonzero, lax.rsqrt(jnp.where(nonzero, dist_sq, 1.0)), 0.0)
    distance = dist_sq * inverse
    inverse_sq = inverse * inverse
    distant = dist_sq >= 4.0 * radius * radius
    iso_distant = 0.75 * radius * inverse * (1.0 + 2.0 / 3.0 * radius * radius * inverse_sq)
    dyad_distant = 0.75 * radius * inverse * (1.0 - 2.0 * radius * radius * inverse_sq) * inverse_sq
    iso_close = 1.0 - 9.0 * distance / (32.0 * radius)
    dyad_close = 3.0 * inverse / (32.0 * radius)
    iso_coef = jnp.where(distant, iso_distant, iso_close)
    dyad_coef = jnp.where(distant, dyad_distant, dyad_close)
    projected = lax.optimization_barrier(jnp.sum(offset * source_force[:, None, :], axis=0))
    return lax.optimization_barrier(jnp.sum(iso_coef[None] * source_force[:, None, :] + (dyad_coef * projected)[None] * offset, axis=2))

def accumulate(target_pos, source_pos, source_force):
    target_count = target_pos.shape[1]
    source_count = source_pos.shape[1]
    target_step = 512 if target_count % 512 == 0 else target_count
    source_step = 512 if source_count % 512 == 0 else 128 if source_count % 128 == 0 else source_count
    target_tiles = target_pos.reshape(3, target_count // target_step, target_step).transpose(1, 0, 2)
    source_tiles = jnp.concatenate([source_pos, source_force], 0).reshape(6, source_count // source_step, source_step).transpose(1, 0, 2)

    def one_target(target_tile):

        def add_tile(carry, source_tile):
            return (carry + pair_sum(target_tile, source_tile[:3], source_tile[3:]), None)
        result, unused = lax.scan(add_tile, jnp.zeros((3, target_step), jnp.float32), source_tiles)
        return result
    result = lax.map(one_target, target_tiles)
    return result.transpose(1, 0, 2).reshape(3, target_count)

def cross_product(left, right):
    return jnp.stack([left[1] * right[2] - left[2] * right[1], left[2] * right[0] - left[0] * right[2], left[0] * right[1] - left[1] * right[0]], 0)

def reference(positions, forces, membership, owner_slot):
    velocity = accumulate(positions, positions, forces)
    slot = owner_slot[membership].astype(jnp.int32)
    moments = jnp.concatenate([velocity, cross_product(positions, velocity), positions], 0)
    totals = jax.ops.segment_sum(moments.T, slot, AGG).T
    counts = jax.ops.segment_sum(jnp.ones_like(positions[0]), slot, AGG)
    centre = totals[6:9] / counts[None, :]
    torque = totals[3:6] - cross_product(centre, totals[0:3])
    rigid = jnp.concatenate([totals[0:3], torque, centre], 0)
    return (velocity, rigid)
```

```python
import functools
import math

import jax
import jax.numpy as jnp
from jax import lax
from jax.experimental import pallas as pl
from jax.experimental.pallas import tpu as pltpu
from jax.sharding import PartitionSpec as P

SCALE = math.sqrt(0.75)
ISO = 9.0 / (32.0 * SCALE)
DYAD = 3.0 * ISO
TOUCH = 2.0 * SCALE
TOUCH_INVERSE = 1.0 / TOUCH
SMALLEST = 1.1754944e-38

LANES = 128
SUBLANES = 8
GROUPS_AT_ONCE = 4
BLOCKS_AT_ONCE = 8
AXES = ("tgt", "src", "sub")


def pair_kernel(own_ref, source_ref, before_ref, out_ref, turned, total):
    count = own_ref.shape[1]
    sources = source_ref.shape[1]
    blocks = sources // LANES
    together = math.gcd(blocks, BLOCKS_AT_ONCE)
    rows = SUBLANES * math.gcd(count // SUBLANES, GROUPS_AT_ONCE)
    groups = rows // SUBLANES

    for start in range(0, count, LANES):
        tile = jnp.concatenate(
            [own_ref[:, start : start + LANES], jnp.zeros((2, LANES), jnp.float32)], axis=0
        )
        turned[start : start + LANES, :] = tile.T

    def target_step(step, unused):
        first = pl.multiple_of(step * rows, rows)
        points = []
        for group in range(groups):
            column = turned[pl.ds(first + group * SUBLANES, SUBLANES), :]
            points.append(
                [jnp.broadcast_to(column[:, k : k + 1], (SUBLANES, LANES)) for k in range(3)]
            )

        def source_step(number, carry):
            sums = [list(one) for one in carry]
            base = number * (together * LANES)
            for block in range(together):
                lanes = pl.ds(pl.multiple_of(base + block * LANES, LANES), LANES)
                x, y, z, fx, fy, fz = [
                    jnp.broadcast_to(source_ref[k : k + 1, lanes], (SUBLANES, LANES))
                    for k in range(6)
                ]
                for group in range(groups):
                    px, py, pz = points[group]
                    dx, dy, dz = px - x, py - y, pz - z
                    square = dx * dx + dy * dy + dz * dz
                    inverse = lax.rsqrt(jnp.maximum(square, SMALLEST))
                    held = jnp.minimum(inverse, TOUCH_INVERSE)
                    held_sq = held * held
                    gap = jnp.maximum(TOUCH - square * inverse, 0.0)
                    iso = held * (held_sq + 2.0) + gap
                    along = dx * fx + dy * fy + dz * fz
                    dyad = (inverse * (held_sq * (2.0 / 3.0 - held_sq))) * along
                    one = sums[group]
                    sums[group] = [
                        one[0] + iso * fx,
                        one[1] + iso * fy,
                        one[2] + iso * fz,
                        one[3] + dyad * dx,
                        one[4] + dyad * dy,
                        one[5] + dyad * dz,
                    ]
            return tuple(tuple(one) for one in sums)

        zero = jnp.zeros((SUBLANES, LANES), jnp.float32)
        carry = tuple((zero,) * 6 for _ in range(groups))
        if blocks == together:
            carry = source_step(0, carry)
        else:
            carry = lax.fori_loop(0, blocks // together, source_step, carry)
        for group in range(groups):
            for k in range(3):
                total[k, pl.ds(first + group * SUBLANES, SUBLANES), :] = (
                    ISO * carry[group][k] + DYAD * carry[group][3 + k]
                )
        return unused

    lax.fori_loop(0, count // rows, target_step, 0)
    ones = jnp.ones((SUBLANES, LANES), jnp.float32)
    for k in range(3):
        summed = lax.dot_general(
            ones,
            total[k],
            (((1,), (1,)), ((), ())),
            precision=lax.Precision.HIGHEST,
            preferred_element_type=jnp.float32,
        )
        out_ref[k : k + 1, :] = before_ref[k : k + 1, :] + summed[0:1, :]


def velocities(own, source, before):
    count, sources = own.shape[1], source.shape[1]
    whole = pl.BlockSpec(memory_space=pltpu.VMEM)
    return pl.pallas_call(
        pair_kernel,
        out_shape=jax.ShapeDtypeStruct((3, count), jnp.float32),
        in_specs=[whole] * 3,
        out_specs=whole,
        scratch_shapes=[
            pltpu.VMEM((count, SUBLANES), jnp.float32),
            pltpu.VMEM((3, count, LANES), jnp.float32),
        ],
        compiler_params=pltpu.CompilerParams(vmem_limit_bytes=16 << 20),
        cost_estimate=pl.CostEstimate(
            flops=40 * count * sources, bytes_accessed=4 * 9 * sources, transcendentals=count * sources
        ),
    )(own, source, before)


def sums_kernel(velocity_ref, position_ref, member_ref, out_ref):
    aggregates = out_ref.shape[1]
    count = velocity_ref.shape[1]
    u = [velocity_ref[k : k + 1, :] for k in range(3)]
    x = [position_ref[k : k + 1, :] for k in range(3)]
    moments = jnp.concatenate(
        u
        + [
            x[1] * u[2] - x[2] * u[1],
            x[2] * u[0] - x[0] * u[2],
            x[0] * u[1] - x[1] * u[0],
        ]
        + x
        + [jnp.ones((1, count), jnp.float32)]
        + [jnp.zeros((6, count), jnp.float32)],
        axis=0,
    )
    labels = lax.broadcasted_iota(jnp.int32, (aggregates, count), 0)
    matches = jnp.where(labels == member_ref[...], 1.0, 0.0)
    out_ref[...] = lax.dot_general(
        moments,
        matches,
        (((1,), (1,)), ((), ())),
        precision=lax.Precision.HIGHEST,
        preferred_element_type=jnp.float32,
    )


def aggregate_sums(velocity, positions, membership, aggregates):
    whole = pl.BlockSpec(memory_space=pltpu.VMEM)
    return pl.pallas_call(
        sums_kernel,
        out_shape=jax.ShapeDtypeStruct((16, aggregates), jnp.float32),
        in_specs=[whole] * 3,
        out_specs=whole,
        compiler_params=pltpu.CompilerParams(vmem_limit_bytes=16 << 20),
    )(velocity, positions, membership[None, :])


def rigid_kernel(first_ref, sums_ref, owner_ref, out_ref):
    columns = out_ref.shape[1]
    sums = sums_ref[...]
    for column in range(columns):
        chosen = owner_ref[...] == first_ref[0] + column
        mine = jnp.sum(jnp.where(chosen, sums, 0.0), axis=1, keepdims=True)
        u = [mine[k : k + 1] for k in range(3)]
        moment = [mine[3 + k : 4 + k] for k in range(3)]
        centre = [mine[6 + k : 7 + k] / mine[9:10] for k in range(3)]
        torque = [
            moment[0] - (centre[1] * u[2] - centre[2] * u[1]),
            moment[1] - (centre[2] * u[0] - centre[0] * u[2]),
            moment[2] - (centre[0] * u[1] - centre[1] * u[0]),
        ]
        for row, value in enumerate(u + torque + centre):
            out_ref[row : row + 1, column : column + 1] = value


def rigid_columns(first, sums, owner_slot, columns):
    whole = pl.BlockSpec(memory_space=pltpu.VMEM)
    return pl.pallas_call(
        rigid_kernel,
        out_shape=jax.ShapeDtypeStruct((9, columns), jnp.float32),
        in_specs=[pl.BlockSpec(memory_space=pltpu.SMEM), whole, whole],
        out_specs=whole,
        compiler_params=pltpu.CompilerParams(vmem_limit_bytes=16 << 20),
    )(first, sums, owner_slot[None, :])


def exchange_steps(mesh):
    steps = []
    for axis in reversed(AXES):
        size = mesh.shape[axis]
        reach = 1
        while reach < size:
            steps.append((axis, [(i, i ^ reach) for i in range(size)]))
            reach *= 2
    return steps


def on_device(steps, devices, positions, forces, membership, owner_slot):
    own = jnp.concatenate([SCALE * positions, forces], axis=0)
    velocity = jnp.zeros_like(positions)
    held, arrived = own, own
    for axis, pairs in steps:
        coming = lax.ppermute(held, axis, pairs)
        velocity = velocities(own, arrived, velocity)
        velocity, coming = lax.optimization_barrier((velocity, coming))
        held, arrived = jnp.concatenate([held, coming], axis=1), coming
    velocity = velocities(own, arrived, velocity)

    aggregates = owner_slot.shape[0]
    sums = aggregate_sums(velocity, positions, membership, aggregates)
    for axis, pairs in steps:
        sums = sums + lax.ppermute(sums, axis, pairs)
    columns = aggregates // devices
    first = (lax.axis_index(AXES) * columns).astype(jnp.int32).reshape(1)
    return velocity, rigid_columns(first, sums, owner_slot, columns)


def solution(mesh):
    placed = (
        P(None, ("groups",) + AXES),
        P(None, ("groups",) + AXES),
        P(("groups",) + AXES),
        P("groups"),
    )
    devices = math.prod(mesh.shape[axis] for axis in AXES)
    return jax.shard_map(
        functools.partial(on_device, exchange_steps(mesh), devices),
        mesh=mesh,
        in_specs=placed,
        out_specs=(P(None, ("groups",) + AXES), P(None, ("groups",) + AXES)),
        check_vma=False,
    )
```

```python
import functools
import math

import jax
import jax.numpy as jnp
from jax import lax
from jax.experimental import pallas as pl
from jax.experimental.pallas import tpu as pltpu
from jax.sharding import PartitionSpec as P

SCALE = math.sqrt(0.75)
ISO = 9.0 / (32.0 * SCALE)
DYAD = 3.0 * ISO
TOUCH = 2.0 * SCALE
TOUCH_INVERSE = 1.0 / TOUCH
SMALLEST = 1.1754944e-38

LANES = 128
SUBLANES = 8
GROUPS_AT_ONCE = 2
BLOCKS_AT_ONCE = 16
AXES = ("tgt", "src", "sub")
NEAR = 1.0 / ISO


def add_pairs(points_ref, source_ref, before_ref, total_ref):
    count = points_ref.shape[1]
    blocks = source_ref.shape[1] // LANES
    together = math.gcd(blocks, BLOCKS_AT_ONCE)
    groups = math.gcd(count // SUBLANES, GROUPS_AT_ONCE)
    rows = SUBLANES * groups

    def target_step(step, unused):
        first = pl.multiple_of(step * rows, rows)
        slices = [pl.ds(first + group * SUBLANES, SUBLANES) for group in range(groups)]
        points = [[points_ref[k, one, :] for k in range(3)] for one in slices]

        def source_step(number, carry):
            sums = [list(one) for one in carry]
            base = number * (together * LANES)
            for block in range(together):
                lanes = pl.ds(pl.multiple_of(base + block * LANES, LANES), LANES)
                x, y, z, fx, fy, fz = [
                    jnp.broadcast_to(source_ref[k : k + 1, lanes], (SUBLANES, LANES))
                    for k in range(6)
                ]
                for group in range(groups):
                    px, py, pz = points[group]
                    dx, dy, dz = px - x, py - y, pz - z
                    square = dx * dx + dy * dy + dz * dz
                    inverse = lax.rsqrt(jnp.maximum(square, SMALLEST))
                    held = jnp.minimum(inverse, TOUCH_INVERSE)
                    held_sq = held * held
                    iso = jnp.maximum(held * (held_sq + 2.0), NEAR - square * inverse)
                    along = dx * fx + dy * fy + dz * fz
                    dyad = (inverse * (held_sq * (2.0 / 3.0 - held_sq))) * along
                    one = sums[group]
                    sums[group] = [
                        one[0] + iso * fx,
                        one[1] + iso * fy,
                        one[2] + iso * fz,
                        one[3] + dyad * dx,
                        one[4] + dyad * dy,
                        one[5] + dyad * dz,
                    ]
            return tuple(tuple(one) for one in sums)

        zero = jnp.zeros((SUBLANES, LANES), jnp.float32)
        carry = tuple((zero,) * 6 for _ in range(groups))
        if blocks == together:
            carry = source_step(0, carry)
        else:
            carry = lax.fori_loop(0, blocks // together, source_step, carry)
        for group in range(groups):
            for k in range(3):
                value = ISO * carry[group][k] + DYAD * carry[group][3 + k]
                if before_ref is not None:
                    value = before_ref[k, slices[group], :] + value
                total_ref[k, slices[group], :] = value
        return unused

    lax.fori_loop(0, count // rows, target_step, 0)


def first_kernel(
    own_ref, position_ref, member_ref, owner_ref, points_ref, total_ref, match_ref, kept_ref
):
    count = own_ref.shape[1]
    for start in range(0, count, LANES):
        tile = jnp.concatenate(
            [own_ref[:, start : start + LANES], jnp.zeros((2, LANES), jnp.float32)], axis=0
        ).T
        for k in range(3):
            points_ref[k, start : start + LANES, :] = jnp.broadcast_to(
                tile[:, k : k + 1], (LANES, LANES)
            )
    aggregates = match_ref.shape[0]
    labels = lax.broadcasted_iota(jnp.int32, (aggregates, count), 0)
    member = jnp.where(labels == member_ref[...], 1.0, 0.0).astype(jnp.bfloat16)
    columns = lax.broadcasted_iota(jnp.int32, (aggregates, aggregates), 0)
    owner = jnp.where(columns == owner_ref[...], 1.0, 0.0).astype(jnp.bfloat16)
    match_ref[...] = jnp.dot(owner, member, preferred_element_type=jnp.float32).astype(
        jnp.bfloat16
    )
    kept_ref[...] = position_ref[...]
    add_pairs(points_ref, own_ref, None, total_ref)


def middle_kernel(points_ref, source_ref, before_ref, total_ref):
    add_pairs(points_ref, source_ref, before_ref, total_ref)


def last_kernel(
    points_ref, source_ref, before_ref, match_ref, kept_ref, velocity_ref, sums_ref, total
):
    add_pairs(points_ref, source_ref, before_ref, total)
    count = points_ref.shape[1]
    u = []
    for k in range(3):
        parts = [
            jnp.sum(total[k, start : start + LANES, :].T, axis=0, keepdims=True)
            for start in range(0, count, LANES)
        ]
        u.append(jnp.concatenate(parts, axis=1))
        velocity_ref[k : k + 1, :] = u[k]
    x = [kept_ref[k : k + 1, :] for k in range(3)]
    moments = jnp.concatenate(
        u
        + [
            x[1] * u[2] - x[2] * u[1],
            x[2] * u[0] - x[0] * u[2],
            x[0] * u[1] - x[1] * u[0],
        ]
        + x
        + [jnp.ones((1, count), jnp.float32), jnp.zeros((6, count), jnp.float32)],
        axis=0,
    )
    parts, rest = [], moments
    for _ in range(3):
        part = rest.astype(jnp.bfloat16)
        rest = rest - part.astype(jnp.float32)
        parts.append(part)
    summed = [
        lax.dot_general(
            part,
            match_ref[...],
            (((1,), (1,)), ((), ())),
            preferred_element_type=jnp.float32,
        )
        for part in parts
    ]
    sums_ref[...] = (summed[2] + summed[1]) + summed[0]


def rigid_kernel(first_ref, sums_ref, out_ref):
    columns = out_ref.shape[0]
    sums = sums_ref[...]
    lane = lax.broadcasted_iota(jnp.int32, sums.shape, 1)
    for column in range(columns):
        chosen = lane == first_ref[0] + column
        mine = jnp.sum(jnp.where(chosen, sums, 0.0), axis=1, keepdims=True)
        u = [mine[k : k + 1] for k in range(3)]
        moment = [mine[3 + k : 4 + k] for k in range(3)]
        centre = [mine[6 + k : 7 + k] / mine[9:10] for k in range(3)]
        torque = [
            moment[0] - (centre[1] * u[2] - centre[2] * u[1]),
            moment[1] - (centre[2] * u[0] - centre[0] * u[2]),
            moment[2] - (centre[0] * u[1] - centre[1] * u[0]),
        ]
        for row, value in enumerate(u + torque + centre):
            out_ref[column : column + 1, row : row + 1] = value


WHOLE = pl.BlockSpec(memory_space=pltpu.VMEM)


def call(kernel, shapes, arguments, pairs=0, scratch=(), specs=None, aliases={}):
    return pl.pallas_call(
        kernel,
        out_shape=[jax.ShapeDtypeStruct(shape, dtype) for shape, dtype in shapes],
        in_specs=specs or [WHOLE] * len(arguments),
        out_specs=[WHOLE] * len(shapes),
        scratch_shapes=list(scratch),
        input_output_aliases=aliases,
        compiler_params=pltpu.CompilerParams(vmem_limit_bytes=16 << 20),
        cost_estimate=pl.CostEstimate(
            flops=40 * pairs + 1000, bytes_accessed=1000, transcendentals=pairs
        ),
    )(*arguments)


def exchange_steps(mesh):
    steps = []
    for axis in reversed(AXES):
        size = mesh.shape[axis]
        reach = 1
        while reach < size:
            steps.append((axis, [(i, i ^ reach) for i in range(size)]))
            reach *= 2
    return steps


def on_device(steps, devices, positions, forces, membership, owner_slot):
    count, aggregates = positions.shape[1], owner_slot.shape[0]
    real = jnp.float32
    own = jnp.concatenate([SCALE * positions, forces], axis=0)
    wide = ((3, count, LANES), real)
    held, arrived = own, own
    for number, (axis, pairs) in enumerate(steps):
        coming = lax.ppermute(held, axis, pairs)
        if number == 0:
            points, total, match, kept = call(
                first_kernel,
                [wide, wide, ((aggregates, count), jnp.bfloat16), ((3, count), real)],
                (own, positions, membership[None, :], owner_slot[None, :]),
                pairs=count * count,
            )
        else:
            (total,) = call(
                middle_kernel,
                [wide],
                (points, arrived, total),
                pairs=count * arrived.shape[1],
                aliases={2: 0},
            )
        total, coming = lax.optimization_barrier((total, coming))
        held, arrived = jnp.concatenate([held, coming], axis=1), coming
    velocity, sums = call(
        last_kernel,
        [((3, count), real), ((16, aggregates), real)],
        (points, arrived, total, match, kept),
        pairs=count * arrived.shape[1],
        scratch=[pltpu.VMEM((3, count, LANES), real)],
    )
    for axis, pairs in steps:
        sums = sums + lax.ppermute(sums, axis, pairs)
    columns = aggregates // devices
    first = (lax.axis_index(AXES) * columns).astype(jnp.int32).reshape(1)
    (rigid,) = call(
        rigid_kernel,
        [((columns, 9), real)],
        (first, sums),
        specs=[pl.BlockSpec(memory_space=pltpu.SMEM), WHOLE],
    )
    return velocity, rigid.T


def solution(mesh):
    placed = (
        P(None, ("groups",) + AXES),
        P(None, ("groups",) + AXES),
        P(("groups",) + AXES),
        P("groups"),
    )
    devices = math.prod(mesh.shape[axis] for axis in AXES)
    return jax.shard_map(
        functools.partial(on_device, exchange_steps(mesh), devices),
        mesh=mesh,
        in_specs=placed,
        out_specs=(P(None, ("groups",) + AXES), P(None, ("groups",) + AXES)),
        check_vma=False,
    )
```

```python
import functools
import math

import jax
import jax.numpy as jnp
from jax import lax
from jax.experimental import pallas as pl
from jax.experimental.pallas import tpu as pltpu
from jax.sharding import PartitionSpec as P

SCALE = math.sqrt(0.75)
ISO = 9.0 / (32.0 * SCALE)
DYAD = 3.0 * ISO
NEAR = 1.0 / ISO
TOUCH_INVERSE = 1.0 / (2.0 * SCALE)
SMALLEST = 1.1754944e-38

LANES = 128
SUBLANES = 8
GROUPS_AT_ONCE = 8
BLOCKS_AT_ONCE = 16
SUM_ROWS = 16
SOURCE_AXES = ("tgt",)
TARGET_AXES = ("sub", "src")
AXES = ("tgt", "src", "sub")


def add_pairs(points_ref, source_ref, before_ref, total_ref, scaled):
    count = points_ref.shape[1]
    blocks = source_ref.shape[1] // LANES
    together = math.gcd(blocks, BLOCKS_AT_ONCE)
    groups = math.gcd(count // SUBLANES, GROUPS_AT_ONCE)
    rows = SUBLANES * groups
    scaled[0:3, :] = SCALE * source_ref[0:3, :]
    scaled[3:6, :] = source_ref[3:6, :]

    def target_step(step, unused):
        first = pl.multiple_of(step * rows, rows)
        slices = [pl.ds(first + group * SUBLANES, SUBLANES) for group in range(groups)]
        points = [[points_ref[k, one, :] for k in range(3)] for one in slices]

        def source_step(number, carry):
            sums = [list(one) for one in carry]
            base = number * (together * LANES)
            for block in range(together):
                lanes = pl.ds(pl.multiple_of(base + block * LANES, LANES), LANES)
                x, y, z, fx, fy, fz = [
                    jnp.broadcast_to(scaled[k : k + 1, lanes], (SUBLANES, LANES))
                    for k in range(6)
                ]
                for group in range(groups):
                    px, py, pz = points[group]
                    dx, dy, dz = px - x, py - y, pz - z
                    square = dx * dx + dy * dy + dz * dz
                    inverse = lax.rsqrt(jnp.maximum(square, SMALLEST))
                    held = jnp.minimum(inverse, TOUCH_INVERSE)
                    held_sq = held * held
                    iso = jnp.maximum(held * (held_sq + 2.0), NEAR - square * inverse)
                    along = dx * fx + dy * fy + dz * fz
                    dyad = (inverse * (held_sq * (2.0 / 3.0 - held_sq))) * along
                    one = sums[group]
                    sums[group] = [
                        one[0] + iso * fx,
                        one[1] + iso * fy,
                        one[2] + iso * fz,
                        one[3] + dyad * dx,
                        one[4] + dyad * dy,
                        one[5] + dyad * dz,
                    ]
            return tuple(tuple(one) for one in sums)

        zero = jnp.zeros((SUBLANES, LANES), jnp.float32)
        carry = tuple((zero,) * 6 for _ in range(groups))
        if blocks == together:
            carry = source_step(0, carry)
        else:
            carry = lax.fori_loop(0, blocks // together, source_step, carry)
        for group in range(groups):
            for k in range(3):
                value = ISO * carry[group][k] + DYAD * carry[group][3 + k]
                if before_ref is not None:
                    value = before_ref[k, slices[group], :] + value
                total_ref[k, slices[group], :] = value
        return unused

    lax.fori_loop(0, count // rows, target_step, 0)


def head_kernel(
    position_in,
    force_in,
    member_in,
    owner_in,
    source_ref,
    target_ref,
    owner_ref,
    position,
    force,
    member,
    arrived,
):
    moves = [(position_in, position), (force_in, force), (member_in, member), (owner_in, owner_ref)]
    copies = [
        pltpu.make_async_copy(there, here, arrived.at[number])
        for number, (there, here) in enumerate(moves)
    ]
    for copy in copies:
        copy.start()
    for copy in copies:
        copy.wait()
    source_ref[0:3, :] = position[...]
    source_ref[3:6, :] = force[...]
    target_ref[0:3, :] = position[...]
    target_ref[3:4, :] = member[...].astype(jnp.float32)


def first_kernel(target_ref, source_ref, owner_ref, points_ref, total_ref, match_ref, scaled):
    count = target_ref.shape[1]
    for start in range(0, count, LANES):
        tile = jnp.concatenate(
            [target_ref[:, start : start + LANES], jnp.zeros((4, LANES), jnp.float32)], axis=0
        )
        turned = (SCALE * tile).T
        for k in range(3):
            points_ref[k, start : start + LANES, :] = jnp.broadcast_to(
                turned[:, k : k + 1], (LANES, LANES)
            )
    aggregates = match_ref.shape[0]
    labels = lax.broadcasted_iota(jnp.int32, (aggregates, count), 0)
    member = jnp.where(labels == target_ref[3:4, :].astype(jnp.int32), 1.0, 0.0)
    columns = lax.broadcasted_iota(jnp.int32, (aggregates, aggregates), 0)
    owner = jnp.where(columns == owner_ref[...], 1.0, 0.0)
    match_ref[...] = jnp.dot(
        owner.astype(jnp.bfloat16),
        member.astype(jnp.bfloat16),
        preferred_element_type=jnp.float32,
    ).astype(jnp.bfloat16)
    add_pairs(points_ref, source_ref, None, total_ref, scaled)


def last_kernel(
    unit_count,
    points_ref,
    source_ref,
    before_ref,
    match_ref,
    target_ref,
    keep_ref,
    send_ref,
    total,
    scaled,
):
    add_pairs(points_ref, source_ref, before_ref, total, scaled)
    count = points_ref.shape[1]
    aggregates = match_ref.shape[0]
    per_unit, units = unit_count // LANES, count // unit_count
    first_row, unit_rows = sum_rows(aggregates), velocity_rows(unit_count)
    keep_ref[...] = jnp.zeros_like(keep_ref)
    send_ref[...] = jnp.zeros_like(send_ref)
    u = []
    for k in range(3):
        parts = []
        for tile in range(count // LANES):
            part = jnp.sum(
                total[k, tile * LANES : (tile + 1) * LANES, :].T, axis=0, keepdims=True
            )
            parts.append(part)
            unit, block = divmod(tile, per_unit)
            packed, unit = (keep_ref, unit) if unit < units // 2 else (send_ref, unit - units // 2)
            row = first_row + unit * unit_rows + k * per_unit + block
            packed[row : row + 1, :] = part
        u.append(jnp.concatenate(parts, axis=1))
    x = [target_ref[k : k + 1, :] for k in range(3)]
    moments = jnp.concatenate(
        u
        + [
            x[1] * u[2] - x[2] * u[1],
            x[2] * u[0] - x[0] * u[2],
            x[0] * u[1] - x[1] * u[0],
        ]
        + x
        + [jnp.ones((1, count), jnp.float32), jnp.zeros((SUM_ROWS - 10, count), jnp.float32)],
        axis=0,
    )
    parts, rest = [], moments
    for _ in range(3):
        part = rest.astype(jnp.bfloat16)
        rest = rest - part.astype(jnp.float32)
        parts.append(part)
    summed = [
        lax.dot_general(
            part,
            match_ref[...],
            (((1,), (1,)), ((), ())),
            preferred_element_type=jnp.float32,
        )
        for part in parts
    ]
    sums = (summed[2] + summed[1]) + summed[0]
    for chunk, start in enumerate(range(0, aggregates, LANES)):
        width = min(LANES, aggregates - start)
        for packed in (keep_ref, send_ref):
            packed[chunk * SUM_ROWS : (chunk + 1) * SUM_ROWS, 0:width] = sums[
                :, start : start + width
            ]


def velocity_kernel(packed_ref, out_ref):
    per_unit = out_ref.shape[1] // LANES
    for k in range(3):
        for block in range(per_unit):
            row = k * per_unit + block
            out_ref[k : k + 1, block * LANES : (block + 1) * LANES] = packed_ref[row : row + 1, :]


def rigid_kernel(first_ref, sums_ref, out_ref):
    columns = out_ref.shape[0]
    lane = lax.broadcasted_iota(jnp.int32, (SUM_ROWS, LANES), 1)
    for column in range(columns):
        wanted = first_ref[0] + column
        mine = jnp.zeros((SUM_ROWS, LANES), jnp.float32)
        for chunk in range(sums_ref.shape[0] // SUM_ROWS):
            sums = sums_ref[chunk * SUM_ROWS : (chunk + 1) * SUM_ROWS, :]
            mine = jnp.where(lane + chunk * LANES == wanted, sums, mine)
        mine = jnp.where(lane == wanted % LANES, mine, 0.0)
        mine = jnp.sum(mine, axis=1, keepdims=True)
        u = [mine[k : k + 1] for k in range(3)]
        moment = [mine[3 + k : 4 + k] for k in range(3)]
        centre = [mine[6 + k : 7 + k] / mine[9:10] for k in range(3)]
        torque = [
            moment[0] - (centre[1] * u[2] - centre[2] * u[1]),
            moment[1] - (centre[2] * u[0] - centre[0] * u[2]),
            moment[2] - (centre[0] * u[1] - centre[1] * u[0]),
        ]
        for row, value in enumerate(u + torque + centre):
            out_ref[column : column + 1, row : row + 1] = value


def sum_rows(aggregates):
    return SUM_ROWS * pl.cdiv(aggregates, LANES)


def velocity_rows(count):
    return SUBLANES * pl.cdiv(3 * (count // LANES), SUBLANES)


WHOLE = pl.BlockSpec(memory_space=pltpu.VMEM)


def call(kernel, shapes, arguments, pairs=0, scratch=(), specs=None, vmem=8 << 20):
    return pl.pallas_call(
        kernel,
        out_shape=[jax.ShapeDtypeStruct(shape, dtype) for shape, dtype in shapes],
        in_specs=specs or [WHOLE] * len(arguments),
        out_specs=[WHOLE] * len(shapes),
        scratch_shapes=list(scratch),
        compiler_params=pltpu.CompilerParams(vmem_limit_bytes=vmem),
        cost_estimate=pl.CostEstimate(
            flops=40 * pairs + 1000, bytes_accessed=1000, transcendentals=pairs
        ),
    )(*arguments)


def doubling(mesh, axes):
    steps = []
    for axis in axes:
        size = mesh.shape[axis]
        reach = 1
        while reach < size:
            steps.append((axis, [(i, i ^ reach) for i in range(size)]))
            reach *= 2
    return steps


def on_device(source_steps, target_steps, devices, positions, forces, membership, owner_slot):
    count, aggregates = positions.shape[1], owner_slot.shape[0]
    real = jnp.float32
    sources, targets, owner = call(
        head_kernel,
        [((6, count), real), ((4, count), real), ((1, aggregates), jnp.int32)],
        [
            pltpu.with_memory_space_constraint(one, pltpu.HBM)
            for one in (positions, forces, membership[None, :], owner_slot[None, :])
        ],
        scratch=[
            pltpu.VMEM((3, count), real),
            pltpu.VMEM((3, count), real),
            pltpu.VMEM((1, count), jnp.int32),
            pltpu.SemaphoreType.DMA((4,)),
        ],
        specs=[pl.BlockSpec(memory_space=pltpu.HBM)] * 4,
    )

    coming = None
    for number in range(max(len(source_steps), len(target_steps))):
        if number < len(target_steps):
            axis, pairs = target_steps[number]
            targets = jnp.concatenate([targets, lax.ppermute(targets, axis, pairs)], axis=1)
        if number < len(source_steps):
            if coming is not None:
                sources = jnp.concatenate([sources, coming], axis=1)
            axis, pairs = source_steps[number]
            coming = lax.ppermute(sources, axis, pairs)
    seen = targets.shape[1]
    wide = ((3, seen, LANES), real)
    scaled = pltpu.VMEM((SUBLANES, sources.shape[1]), real)
    vmem = (8 << 20) + 4 * (4 * 3 * seen * LANES)
    points, total, match = call(
        first_kernel,
        [wide, wide, ((aggregates, seen), jnp.bfloat16)],
        (targets, sources, owner),
        pairs=seen * sources.shape[1],
        scratch=[scaled],
        vmem=vmem,
    )
    total, coming = lax.optimization_barrier((total, coming))
    first_row, units = sum_rows(aggregates), seen // count
    unit_rows = velocity_rows(count)
    packed = ((first_row + units // 2 * unit_rows, LANES), real)
    keep, send = call(
        functools.partial(last_kernel, count),
        [packed, packed],
        (points, coming, total, match, targets),
        pairs=seen * coming.shape[1],
        scratch=[pltpu.VMEM((3, seen, LANES), real), scaled],
        vmem=vmem,
    )

    for axis, pairs in reversed(target_steps):
        if keep is None:
            half = (both.shape[0] - first_row) // 2
            keep = both[: first_row + half]
            send = jnp.concatenate([both[:first_row], both[first_row + half :]], axis=0)
        both = keep + lax.ppermute(send, axis, pairs)
        keep = None
    sums, mine = both[:first_row], both[first_row:]
    for number, (axis, pairs) in enumerate(source_steps):
        coming = lax.ppermute(sums, axis, pairs)
        if number == 0:
            (velocity,) = call(velocity_kernel, [((3, count), real)], (mine,))
            velocity, coming = lax.optimization_barrier((velocity, coming))
        sums = sums + coming
    columns = aggregates // devices
    first = (lax.axis_index(AXES) * columns).astype(jnp.int32).reshape(1)
    (rigid,) = call(
        rigid_kernel,
        [((columns, 9), real)],
        (first, sums),
        specs=[pl.BlockSpec(memory_space=pltpu.SMEM), WHOLE],
    )
    return velocity, rigid.T


def solution(mesh):
    placed = (
        P(None, ("groups",) + AXES),
        P(None, ("groups",) + AXES),
        P(("groups",) + AXES),
        P("groups"),
    )
    devices = math.prod(mesh.shape[axis] for axis in AXES)
    return jax.shard_map(
        functools.partial(
            on_device, doubling(mesh, SOURCE_AXES), doubling(mesh, TARGET_AXES), devices
        ),
        mesh=mesh,
        in_specs=placed,
        out_specs=(P(None, ("groups",) + AXES), P(None, ("groups",) + AXES)),
        check_vma=False,
    )
```

```python
import functools
import math

import jax
import jax.numpy as jnp
from jax import lax
from jax.experimental import pallas as pl
from jax.experimental.pallas import tpu as pltpu
from jax.sharding import PartitionSpec as P

SCALE = math.sqrt(0.75)
ISO = 9.0 / (32.0 * SCALE)
DYAD = 3.0 * ISO
NEAR = 1.0 / ISO
TOUCH_INVERSE = 1.0 / (2.0 * SCALE)
SMALLEST = 1.1754944e-38

LANES = 128
SUBLANES = 8
BLOCKS_AT_ONCE = 4
SUM_ROWS = 16
SOURCE_AXES = ("tgt",)
TARGET_AXES = ("sub", "src")
AXES = ("tgt", "src", "sub")


def add_pairs(points_ref, source_ref, before_ref, total_ref, scaled, beside=None, shift=0):
    count = total_ref.shape[1] - shift
    blocks = source_ref.shape[1] // LANES
    together = math.gcd(blocks, BLOCKS_AT_ONCE)
    scaled[0:3, :] = SCALE * source_ref[0:3, :]
    scaled[3:6, :] = ISO * source_ref[3:6, :]
    scaled[6:9, :] = DYAD * source_ref[3:6, :]

    def add_block(point, base, block, sums):
        lanes = pl.ds(pl.multiple_of(base + block * LANES, LANES), LANES)
        x, y, z, fx, fy, fz, gx, gy, gz = [
            jnp.broadcast_to(scaled[k : k + 1, lanes], (SUBLANES, LANES)) for k in range(9)
        ]
        dx, dy, dz = point[0] - x, point[1] - y, point[2] - z
        square = dx * dx + dy * dy + dz * dz
        inverse = lax.rsqrt(jnp.maximum(square, SMALLEST))
        held = jnp.minimum(inverse, TOUCH_INVERSE)
        held_sq = held * held
        iso = jnp.maximum(held * (held_sq + 2.0), NEAR - square * inverse)
        along = dx * gx + dy * gy + dz * gz
        dyad = (inverse * (held_sq * (2.0 / 3.0 - held_sq))) * along
        terms = (iso * fx + dyad * dx, iso * fy + dyad * dy, iso * fz + dyad * dz)
        return terms if sums is None else tuple(one + term for one, term in zip(sums, terms))

    def tile_step(step, unused):
        first = pl.multiple_of(step * LANES, LANES)
        if beside is not None:
            beside(first)
        for group in range(LANES // SUBLANES):
            rows = pl.ds(first + group * SUBLANES, SUBLANES)
            point = [points_ref[k, rows, :] for k in range(3)]
            sums = None
            if before_ref is not None:
                sums = tuple(before_ref[k, rows, :] for k in range(3))
            if blocks == together:
                for block in range(together):
                    sums = add_block(point, 0, block, sums)
            else:

                def source_step(number, sums):
                    for block in range(together):
                        sums = add_block(point, number * (together * LANES), block, sums)
                    return sums

                zero = jnp.zeros((SUBLANES, LANES), jnp.float32)
                sums = lax.fori_loop(
                    0, blocks // together, source_step, sums or (zero, zero, zero)
                )
            for k in range(3):
                total_ref[k, pl.ds(first + shift + group * SUBLANES, SUBLANES), :] = sums[k]
        return unused

    lax.fori_loop(0, count // LANES, tile_step, 0)


def head_kernel(
    position_in,
    force_in,
    member_in,
    owner_in,
    source_ref,
    target_ref,
    owner_ref,
    position,
    force,
    member,
    arrived,
):
    moves = [(position_in, position), (force_in, force), (member_in, member), (owner_in, owner_ref)]
    copies = [
        pltpu.make_async_copy(there, here, arrived.at[number])
        for number, (there, here) in enumerate(moves)
    ]
    for copy in copies:
        copy.start()
    for copy in copies:
        copy.wait()
    source_ref[0:3, :] = position[...]
    source_ref[3:6, :] = force[...]
    target_ref[0:3, :] = position[...]
    target_ref[3:4, :] = member[...].astype(jnp.float32)


def first_kernel(
    target_ref, source_ref, owner_ref, points_ref, total_ref, match_ref, scaled
):
    count = target_ref.shape[1]
    parts, rest = [], SCALE * target_ref[0:3, :]
    for _ in range(3):
        part = rest.astype(jnp.bfloat16).astype(jnp.float32)
        rest = rest - part
        parts.append(part)
    parts.append(jnp.zeros((7, count), jnp.float32))
    row = lax.broadcasted_iota(jnp.int32, (16, 3 * LANES), 0)
    lane = lax.broadcasted_iota(jnp.int32, (16, 3 * LANES), 1)
    chosen = jnp.where((row % 3 == lane // LANES) & (row < 9), 1.0, 0.0)
    points = lax.dot_general(
        jnp.concatenate(parts, axis=0).astype(jnp.bfloat16),
        chosen.astype(jnp.bfloat16),
        (((0,), (0,)), ((), ())),
        preferred_element_type=jnp.float32,
    )
    for k in range(3):
        points_ref[k, :, :] = points[:, k * LANES : (k + 1) * LANES]
    aggregates = match_ref.shape[0]
    labels = lax.broadcasted_iota(jnp.int32, (aggregates, count), 0)
    member = jnp.where(labels == target_ref[3:4, :].astype(jnp.int32), 1.0, 0.0)
    columns = lax.broadcasted_iota(jnp.int32, (aggregates, aggregates), 0)
    owner = jnp.where(columns == owner_ref[...], 1.0, 0.0)
    match_ref[...] = jnp.dot(
        owner.astype(jnp.bfloat16),
        member.astype(jnp.bfloat16),
        preferred_element_type=jnp.float32,
    ).astype(jnp.bfloat16)

    add_pairs(points_ref, source_ref, None, total_ref, scaled)


def last_kernel(
    unit_count,
    points_ref,
    source_ref,
    before_ref,
    match_ref,
    target_ref,
    keep_ref,
    send_ref,
    total,
    scaled,
    summed,
):
    count = target_ref.shape[1]
    tiles = count // LANES

    def sum_tile(first, tile):
        rows = pl.ds(first, LANES)
        for k in range(3):
            summed[tile, k : k + 1, :] = jnp.sum(total[k, rows, :].T, axis=0, keepdims=True)

    total[:, 0:LANES, :] = jnp.zeros((3, LANES, LANES), jnp.float32)
    add_pairs(
        points_ref,
        source_ref,
        before_ref,
        total,
        scaled,
        lambda first: sum_tile(first, first // LANES),
        LANES,
    )
    sum_tile(count, tiles)

    aggregates = match_ref.shape[0]
    per_unit, units = unit_count // LANES, count // unit_count
    first_row, unit_rows = sum_rows(aggregates), velocity_rows(unit_count)
    keep_ref[...] = jnp.zeros_like(keep_ref)
    send_ref[...] = jnp.zeros_like(send_ref)
    u = []
    for k in range(3):
        parts = [summed[tile + 1, k : k + 1, :] for tile in range(tiles)]
        u.append(jnp.concatenate(parts, axis=1))
        for tile in range(tiles):
            unit, block = divmod(tile, per_unit)
            packed, unit = (keep_ref, unit) if unit < units // 2 else (send_ref, unit - units // 2)
            row = first_row + unit * unit_rows + k * per_unit + block
            packed[row : row + 1, :] = parts[tile]
    x = [target_ref[k : k + 1, :] for k in range(3)]
    moments = jnp.concatenate(
        u
        + [
            x[1] * u[2] - x[2] * u[1],
            x[2] * u[0] - x[0] * u[2],
            x[0] * u[1] - x[1] * u[0],
        ]
        + x
        + [jnp.ones((1, count), jnp.float32), jnp.zeros((SUM_ROWS - 10, count), jnp.float32)],
        axis=0,
    )
    parts, rest = [], moments
    for _ in range(3):
        part = rest.astype(jnp.bfloat16)
        rest = rest - part.astype(jnp.float32)
        parts.append(part)
    products = [
        lax.dot_general(
            part,
            match_ref[...],
            (((1,), (1,)), ((), ())),
            preferred_element_type=jnp.float32,
        )
        for part in parts
    ]
    sums = (products[2] + products[1]) + products[0]
    for chunk, start in enumerate(range(0, aggregates, LANES)):
        width = min(LANES, aggregates - start)
        for packed in (keep_ref, send_ref):
            packed[chunk * SUM_ROWS : (chunk + 1) * SUM_ROWS, 0:width] = sums[
                :, start : start + width
            ]


def velocity_kernel(packed_ref, out_ref):
    per_unit = out_ref.shape[1] // LANES
    for k in range(3):
        for block in range(per_unit):
            row = k * per_unit + block
            out_ref[k : k + 1, block * LANES : (block + 1) * LANES] = packed_ref[row : row + 1, :]


def rigid_kernel(first_ref, sums_ref, out_ref):
    columns = out_ref.shape[0]
    lane = lax.broadcasted_iota(jnp.int32, (SUM_ROWS, LANES), 1)
    for column in range(columns):
        wanted = first_ref[0] + column
        mine = jnp.zeros((SUM_ROWS, LANES), jnp.float32)
        for chunk in range(sums_ref.shape[0] // SUM_ROWS):
            sums = sums_ref[chunk * SUM_ROWS : (chunk + 1) * SUM_ROWS, :]
            mine = jnp.where(lane + chunk * LANES == wanted, sums, mine)
        mine = jnp.where(lane == wanted % LANES, mine, 0.0)
        mine = jnp.sum(mine, axis=1, keepdims=True)
        u = [mine[k : k + 1] for k in range(3)]
        moment = [mine[3 + k : 4 + k] for k in range(3)]
        centre = [mine[6 + k : 7 + k] / mine[9:10] for k in range(3)]
        torque = [
            moment[0] - (centre[1] * u[2] - centre[2] * u[1]),
            moment[1] - (centre[2] * u[0] - centre[0] * u[2]),
            moment[2] - (centre[0] * u[1] - centre[1] * u[0]),
        ]
        for row, value in enumerate(u + torque + centre):
            out_ref[column : column + 1, row : row + 1] = value


def sum_rows(aggregates):
    return SUM_ROWS * pl.cdiv(aggregates, LANES)


def velocity_rows(count):
    return SUBLANES * pl.cdiv(3 * (count // LANES), SUBLANES)


WHOLE = pl.BlockSpec(memory_space=pltpu.VMEM)


def call(kernel, shapes, arguments, pairs=0, scratch=(), specs=None, vmem=8 << 20):
    return pl.pallas_call(
        kernel,
        out_shape=[jax.ShapeDtypeStruct(shape, dtype) for shape, dtype in shapes],
        in_specs=specs or [WHOLE] * len(arguments),
        out_specs=[WHOLE] * len(shapes),
        scratch_shapes=list(scratch),
        compiler_params=pltpu.CompilerParams(vmem_limit_bytes=vmem),
        cost_estimate=pl.CostEstimate(
            flops=40 * pairs + 1000, bytes_accessed=1000, transcendentals=pairs
        ),
    )(*arguments)


def doubling(mesh, axes):
    steps = []
    for axis in axes:
        size = mesh.shape[axis]
        reach = 1
        while reach < size:
            steps.append((axis, [(i, i ^ reach) for i in range(size)]))
            reach *= 2
    return steps


def on_device(source_steps, target_steps, devices, positions, forces, membership, owner_slot):
    count, aggregates = positions.shape[1], owner_slot.shape[0]
    real = jnp.float32
    sources, targets, owner = call(
        head_kernel,
        [((6, count), real), ((4, count), real), ((1, aggregates), jnp.int32)],
        [
            pltpu.with_memory_space_constraint(one, pltpu.HBM)
            for one in (positions, forces, membership[None, :], owner_slot[None, :])
        ],
        scratch=[
            pltpu.VMEM((3, count), real),
            pltpu.VMEM((3, count), real),
            pltpu.VMEM((1, count), jnp.int32),
            pltpu.SemaphoreType.DMA((4,)),
        ],
        specs=[pl.BlockSpec(memory_space=pltpu.HBM)] * 4,
    )

    coming = None
    for number in range(max(len(source_steps), len(target_steps))):
        if number < len(target_steps):
            axis, pairs = target_steps[number]
            targets = jnp.concatenate([targets, lax.ppermute(targets, axis, pairs)], axis=1)
        if number < len(source_steps):
            if coming is not None:
                sources = jnp.concatenate([sources, coming], axis=1)
            axis, pairs = source_steps[number]
            coming = lax.ppermute(sources, axis, pairs)
    seen = targets.shape[1]
    scaled = pltpu.VMEM((2 * SUBLANES, sources.shape[1]), real)
    vmem = (8 << 20) + 4 * (4 * 3 * seen * LANES)
    points, total, match = call(
        first_kernel,
        [
            ((3, seen, LANES), real),
            ((3, seen, LANES), real),
            ((aggregates, seen), jnp.bfloat16),
        ],
        (targets, sources, owner),
        pairs=seen * sources.shape[1],
        scratch=[scaled],
        vmem=vmem,
    )
    total, coming = lax.optimization_barrier((total, coming))
    first_row, units = sum_rows(aggregates), seen // count
    unit_rows = velocity_rows(count)
    packed = ((first_row + units // 2 * unit_rows, LANES), real)
    keep, send = call(
        functools.partial(last_kernel, count),
        [packed, packed],
        (points, coming, total, match, targets),
        pairs=seen * coming.shape[1],
        scratch=[
            pltpu.VMEM((3, seen + LANES, LANES), real),
            scaled,
            pltpu.VMEM((seen // LANES + 1, SUBLANES, LANES), real),
        ],
        vmem=vmem,
    )

    for axis, pairs in reversed(target_steps):
        if keep is None:
            half = (both.shape[0] - first_row) // 2
            keep = both[: first_row + half]
            send = jnp.concatenate([both[:first_row], both[first_row + half :]], axis=0)
        both = keep + lax.ppermute(send, axis, pairs)
        keep = None
    sums, mine = both[:first_row], both[first_row:]
    for number, (axis, pairs) in enumerate(source_steps):
        coming = lax.ppermute(sums, axis, pairs)
        if number == 0:
            (velocity,) = call(velocity_kernel, [((3, count), real)], (mine,))
            velocity, coming = lax.optimization_barrier((velocity, coming))
        sums = sums + coming
    columns = aggregates // devices
    first = (lax.axis_index(AXES) * columns).astype(jnp.int32).reshape(1)
    (rigid,) = call(
        rigid_kernel,
        [((columns, 9), real)],
        (first, sums),
        specs=[pl.BlockSpec(memory_space=pltpu.SMEM), WHOLE],
    )
    return velocity, rigid.T


def solution(mesh):
    placed = (
        P(None, ("groups",) + AXES),
        P(None, ("groups",) + AXES),
        P(("groups",) + AXES),
        P("groups"),
    )
    devices = math.prod(mesh.shape[axis] for axis in AXES)
    return jax.shard_map(
        functools.partial(
            on_device, doubling(mesh, SOURCE_AXES), doubling(mesh, TARGET_AXES), devices
        ),
        mesh=mesh,
        in_specs=placed,
        out_specs=(P(None, ("groups",) + AXES), P(None, ("groups",) + AXES)),
        check_vma=False,
    )
```

```python
import functools
import math

import jax
import jax.numpy as jnp
from jax import lax
from jax.experimental import pallas as pl
from jax.experimental.pallas import tpu as pltpu
from jax.sharding import PartitionSpec as P

SCALE = math.sqrt(0.75)
ISO = 9.0 / (32.0 * SCALE)
DYAD = 3.0 * ISO
NEAR = 1.0 / ISO
TOUCH_INVERSE = 1.0 / (2.0 * SCALE)
SMALLEST = 1.1754944e-38

LANES = 128
SUBLANES = 8
BLOCKS_AT_ONCE = 4
SUM_ROWS = 16
SOURCE_AXES = ("tgt",)
TARGET_AXES = ("sub", "src")
AXES = ("tgt", "src", "sub")


def add_pairs(points_ref, source_ref, before_ref, total_ref, scaled, beside=None, shift=0):
    count = total_ref.shape[1] - shift
    blocks = source_ref.shape[1] // LANES
    together = math.gcd(blocks, BLOCKS_AT_ONCE)
    scaled[0:3, :] = SCALE * source_ref[0:3, :]
    scaled[3:6, :] = ISO * source_ref[3:6, :]
    scaled[6:9, :] = DYAD * source_ref[3:6, :]

    def add_block(point, base, block, sums):
        lanes = pl.ds(pl.multiple_of(base + block * LANES, LANES), LANES)
        x, y, z, fx, fy, fz, gx, gy, gz = [
            jnp.broadcast_to(scaled[k : k + 1, lanes], (SUBLANES, LANES)) for k in range(9)
        ]
        dx, dy, dz = point[0] - x, point[1] - y, point[2] - z
        square = dx * dx + dy * dy + dz * dz
        inverse = lax.rsqrt(jnp.maximum(square, SMALLEST))
        held = jnp.minimum(inverse, TOUCH_INVERSE)
        held_sq = held * held
        iso = jnp.maximum(held * (held_sq + 2.0), NEAR - square * inverse)
        along = dx * gx + dy * gy + dz * gz
        dyad = (inverse * (held_sq * (2.0 / 3.0 - held_sq))) * along
        terms = (iso * fx + dyad * dx, iso * fy + dyad * dy, iso * fz + dyad * dz)
        return terms if sums is None else tuple(one + term for one, term in zip(sums, terms))

    def tile_step(step, unused):
        first = pl.multiple_of(step * LANES, LANES)
        if beside is not None:
            beside(first)
        for group in range(LANES // SUBLANES):
            rows = pl.ds(first + group * SUBLANES, SUBLANES)
            point = [points_ref[k, rows, :] for k in range(3)]
            sums = None
            if before_ref is not None:
                sums = tuple(before_ref[k, rows, :] for k in range(3))
            if blocks == together:
                for block in range(together):
                    sums = add_block(point, 0, block, sums)
            else:

                def source_step(number, sums):
                    for block in range(together):
                        sums = add_block(point, number * (together * LANES), block, sums)
                    return sums

                zero = jnp.zeros((SUBLANES, LANES), jnp.float32)
                sums = lax.fori_loop(
                    0, blocks // together, source_step, sums or (zero, zero, zero)
                )
            for k in range(3):
                total_ref[k, pl.ds(first + shift + group * SUBLANES, SUBLANES), :] = sums[k]
        return unused

    lax.fori_loop(0, count // LANES, tile_step, 0)


def head_kernel(
    position_in,
    force_in,
    member_in,
    owner_in,
    source_ref,
    target_ref,
    owner_ref,
    position,
    force,
    member,
    arrived,
):
    moves = [(position_in, position), (force_in, force), (member_in, member), (owner_in, owner_ref)]
    copies = [
        pltpu.make_async_copy(there, here, arrived.at[number])
        for number, (there, here) in enumerate(moves)
    ]
    for copy in copies:
        copy.start()
    for copy in copies:
        copy.wait()
    source_ref[0:3, :] = position[...]
    source_ref[3:6, :] = force[...]
    target_ref[0:3, :] = position[...]
    target_ref[3:4, :] = member[...].astype(jnp.float32)


def first_kernel(
    target_ref, source_ref, owner_ref, points_ref, total_ref, match_ref, scaled
):
    count = target_ref.shape[1]
    parts, rest = [], SCALE * target_ref[0:3, :]
    for _ in range(3):
        part = rest.astype(jnp.bfloat16).astype(jnp.float32)
        rest = rest - part
        parts.append(part)
    parts.append(jnp.zeros((7, count), jnp.float32))
    row = lax.broadcasted_iota(jnp.int32, (16, 3 * LANES), 0)
    lane = lax.broadcasted_iota(jnp.int32, (16, 3 * LANES), 1)
    chosen = jnp.where((row % 3 == lane // LANES) & (row < 9), 1.0, 0.0)
    points = lax.dot_general(
        jnp.concatenate(parts, axis=0).astype(jnp.bfloat16),
        chosen.astype(jnp.bfloat16),
        (((0,), (0,)), ((), ())),
        preferred_element_type=jnp.float32,
    )
    for k in range(3):
        points_ref[k, :, :] = points[:, k * LANES : (k + 1) * LANES]
    aggregates = match_ref.shape[0]
    labels = lax.broadcasted_iota(jnp.int32, (aggregates, count), 0)
    member = jnp.where(labels == target_ref[3:4, :].astype(jnp.int32), 1.0, 0.0)
    columns = lax.broadcasted_iota(jnp.int32, (aggregates, aggregates), 0)
    owner = jnp.where(columns == owner_ref[...], 1.0, 0.0)
    match_ref[...] = jnp.dot(
        owner.astype(jnp.bfloat16),
        member.astype(jnp.bfloat16),
        preferred_element_type=jnp.float32,
    ).astype(jnp.bfloat16)

    add_pairs(points_ref, source_ref, None, total_ref, scaled)


def last_kernel(
    unit_count,
    points_ref,
    source_ref,
    before_ref,
    match_ref,
    target_ref,
    keep_ref,
    send_ref,
    total,
    scaled,
    summed,
):
    count = target_ref.shape[1]
    tiles = count // LANES

    def sum_tile(first, tile):
        rows = pl.ds(first, LANES)
        for k in range(3):
            summed[tile, k : k + 1, :] = jnp.sum(total[k, rows, :].T, axis=0, keepdims=True)

    total[:, 0:LANES, :] = jnp.zeros((3, LANES, LANES), jnp.float32)
    add_pairs(
        points_ref,
        source_ref,
        before_ref,
        total,
        scaled,
        lambda first: sum_tile(first, first // LANES),
        LANES,
    )
    sum_tile(count, tiles)

    aggregates = match_ref.shape[0]
    per_unit, units = unit_count // LANES, count // unit_count
    first_row, unit_rows = sum_rows(aggregates), velocity_rows(unit_count)
    keep_ref[...] = jnp.zeros_like(keep_ref)
    send_ref[...] = jnp.zeros_like(send_ref)
    u = []
    for k in range(3):
        parts = [summed[tile + 1, k : k + 1, :] for tile in range(tiles)]
        u.append(jnp.concatenate(parts, axis=1))
        for tile in range(tiles):
            unit, block = divmod(tile, per_unit)
            packed, unit = (keep_ref, unit) if unit < units // 2 else (send_ref, unit - units // 2)
            row = first_row + unit * unit_rows + k * per_unit + block
            packed[row : row + 1, :] = parts[tile]
    x = [target_ref[k : k + 1, :] for k in range(3)]
    moments = jnp.concatenate(
        u
        + [
            x[1] * u[2] - x[2] * u[1],
            x[2] * u[0] - x[0] * u[2],
            x[0] * u[1] - x[1] * u[0],
        ]
        + x
        + [jnp.ones((1, count), jnp.float32), jnp.zeros((SUM_ROWS - 10, count), jnp.float32)],
        axis=0,
    )
    parts, rest = [], moments
    for _ in range(3):
        part = rest.astype(jnp.bfloat16)
        rest = rest - part.astype(jnp.float32)
        parts.append(part)
    products = [
        lax.dot_general(
            part,
            match_ref[...],
            (((1,), (1,)), ((), ())),
            preferred_element_type=jnp.float32,
        )
        for part in parts
    ]
    sums = (products[2] + products[1]) + products[0]
    for chunk, start in enumerate(range(0, aggregates, LANES)):
        width = min(LANES, aggregates - start)
        for packed in (keep_ref, send_ref):
            packed[chunk * SUM_ROWS : (chunk + 1) * SUM_ROWS, 0:width] = sums[
                :, start : start + width
            ]


def velocity_kernel(packed_ref, out_ref):
    per_unit = out_ref.shape[1] // LANES
    for k in range(3):
        for block in range(per_unit):
            row = k * per_unit + block
            out_ref[k : k + 1, block * LANES : (block + 1) * LANES] = packed_ref[row : row + 1, :]


def rigid_kernel(first_ref, sums_ref, out_ref):
    columns = out_ref.shape[0]
    lane = lax.broadcasted_iota(jnp.int32, (SUM_ROWS, LANES), 1)
    for column in range(columns):
        wanted = first_ref[0] + column
        mine = jnp.zeros((SUM_ROWS, LANES), jnp.float32)
        for chunk in range(sums_ref.shape[0] // SUM_ROWS):
            sums = sums_ref[chunk * SUM_ROWS : (chunk + 1) * SUM_ROWS, :]
            mine = jnp.where(lane + chunk * LANES == wanted, sums, mine)
        mine = jnp.where(lane == wanted % LANES, mine, 0.0)
        mine = jnp.sum(mine, axis=1, keepdims=True)
        u = [mine[k : k + 1] for k in range(3)]
        moment = [mine[3 + k : 4 + k] for k in range(3)]
        centre = [mine[6 + k : 7 + k] / mine[9:10] for k in range(3)]
        torque = [
            moment[0] - (centre[1] * u[2] - centre[2] * u[1]),
            moment[1] - (centre[2] * u[0] - centre[0] * u[2]),
            moment[2] - (centre[0] * u[1] - centre[1] * u[0]),
        ]
        for row, value in enumerate(u + torque + centre):
            out_ref[column : column + 1, row : row + 1] = value


def sum_rows(aggregates):
    return SUM_ROWS * pl.cdiv(aggregates, LANES)


def velocity_rows(count):
    return SUBLANES * pl.cdiv(3 * (count // LANES), SUBLANES)


WHOLE = pl.BlockSpec(memory_space=pltpu.VMEM)


def call(kernel, shapes, arguments, pairs=0, scratch=(), specs=None, vmem=8 << 20):
    return pl.pallas_call(
        kernel,
        out_shape=[jax.ShapeDtypeStruct(shape, dtype) for shape, dtype in shapes],
        in_specs=specs or [WHOLE] * len(arguments),
        out_specs=[WHOLE] * len(shapes),
        scratch_shapes=list(scratch),
        compiler_params=pltpu.CompilerParams(vmem_limit_bytes=vmem),
        cost_estimate=pl.CostEstimate(
            flops=40 * pairs + 1000, bytes_accessed=1000, transcendentals=pairs
        ),
    )(*arguments)


def doubling(mesh, axes):
    steps = []
    cores = mesh.shape["sub"]
    other = 1 if cores == 2 else 0
    for axis in axes:
        size = mesh.shape[axis]
        reach = 1
        while reach < size:
            if axis == "sub":
                steps.append((axis, [(i, i ^ reach) for i in range(size)]))
            else:
                flip = reach * cores + other
                steps.append(((axis, "sub"), [(i, i ^ flip) for i in range(size * cores)]))
            reach *= 2
    return steps


def on_device(source_steps, target_steps, devices, positions, forces, membership, owner_slot):
    count, aggregates = positions.shape[1], owner_slot.shape[0]
    real = jnp.float32
    sources, targets, owner = call(
        head_kernel,
        [((6, count), real), ((4, count), real), ((1, aggregates), jnp.int32)],
        [
            pltpu.with_memory_space_constraint(one, pltpu.HBM)
            for one in (positions, forces, membership[None, :], owner_slot[None, :])
        ],
        scratch=[
            pltpu.VMEM((3, count), real),
            pltpu.VMEM((3, count), real),
            pltpu.VMEM((1, count), jnp.int32),
            pltpu.SemaphoreType.DMA((4,)),
        ],
        specs=[pl.BlockSpec(memory_space=pltpu.HBM)] * 4,
    )

    coming = None
    for number in range(max(len(source_steps), len(target_steps))):
        if number < len(target_steps):
            axis, pairs = target_steps[number]
            targets = jnp.concatenate([targets, lax.ppermute(targets, axis, pairs)], axis=1)
        if number < len(source_steps):
            if coming is not None:
                sources = jnp.concatenate([sources, coming], axis=1)
            axis, pairs = source_steps[number]
            coming = lax.ppermute(sources, axis, pairs)
    seen = targets.shape[1]
    scaled = pltpu.VMEM((2 * SUBLANES, sources.shape[1]), real)
    vmem = (8 << 20) + 4 * (4 * 3 * seen * LANES)
    points, total, match = call(
        first_kernel,
        [
            ((3, seen, LANES), real),
            ((3, seen, LANES), real),
            ((aggregates, seen), jnp.bfloat16),
        ],
        (targets, sources, owner),
        pairs=seen * sources.shape[1],
        scratch=[scaled],
        vmem=vmem,
    )
    total, coming = lax.optimization_barrier((total, coming))
    first_row, units = sum_rows(aggregates), seen // count
    unit_rows = velocity_rows(count)
    packed = ((first_row + units // 2 * unit_rows, LANES), real)
    keep, send = call(
        functools.partial(last_kernel, count),
        [packed, packed],
        (points, coming, total, match, targets),
        pairs=seen * coming.shape[1],
        scratch=[
            pltpu.VMEM((3, seen + LANES, LANES), real),
            scaled,
            pltpu.VMEM((seen // LANES + 1, SUBLANES, LANES), real),
        ],
        vmem=vmem,
    )

    for axis, pairs in reversed(target_steps):
        if keep is None:
            half = (both.shape[0] - first_row) // 2
            keep = both[: first_row + half]
            send = jnp.concatenate([both[:first_row], both[first_row + half :]], axis=0)
        both = keep + lax.ppermute(send, axis, pairs)
        keep = None
    sums, mine = both[:first_row], both[first_row:]
    for number, (axis, pairs) in enumerate(source_steps):
        coming = lax.ppermute(sums, axis, pairs)
        if number == 0:
            (velocity,) = call(velocity_kernel, [((3, count), real)], (mine,))
            velocity, coming = lax.optimization_barrier((velocity, coming))
        sums = sums + coming
    columns = aggregates // devices
    first = (lax.axis_index(AXES) * columns).astype(jnp.int32).reshape(1)
    (rigid,) = call(
        rigid_kernel,
        [((columns, 9), real)],
        (first, sums),
        specs=[pl.BlockSpec(memory_space=pltpu.SMEM), WHOLE],
    )
    return velocity, rigid.T


def solution(mesh):
    placed = (
        P(None, ("groups",) + AXES),
        P(None, ("groups",) + AXES),
        P(("groups",) + AXES),
        P("groups"),
    )
    devices = math.prod(mesh.shape[axis] for axis in AXES)
    return jax.shard_map(
        functools.partial(
            on_device, doubling(mesh, SOURCE_AXES), doubling(mesh, TARGET_AXES), devices
        ),
        mesh=mesh,
        in_specs=placed,
        out_specs=(P(None, ("groups",) + AXES), P(None, ("groups",) + AXES)),
        check_vma=False,
    )
```

```python
import functools
import math

import jax
import jax.numpy as jnp
from jax import lax
from jax.experimental import pallas as pl
from jax.experimental.pallas import tpu as pltpu
from jax.sharding import PartitionSpec as P

SCALE = math.sqrt(0.75)
ISO = 9.0 / (32.0 * SCALE)
DYAD = 3.0 * ISO
NEAR = 1.0 / ISO
TOUCH_INVERSE = 1.0 / (2.0 * SCALE)
SMALLEST = 1.1754944e-38

LANES = 128
SUBLANES = 8
BLOCKS_AT_ONCE = 4
SUM_ROWS = 16
SOURCE_AXES = ("tgt",)
TARGET_AXES = ("sub", "src")
AXES = ("tgt", "src", "sub")


def add_pairs(points_ref, source_ref, before_ref, total_ref, scaled, beside=None, shift=0):
    count = total_ref.shape[1] - shift
    blocks = source_ref.shape[1] // LANES
    together = math.gcd(blocks, BLOCKS_AT_ONCE)
    scaled[0:3, :] = SCALE * source_ref[0:3, :]
    scaled[3:6, :] = ISO * source_ref[3:6, :]
    scaled[6:9, :] = DYAD * source_ref[3:6, :]

    def add_block(point, base, block, sums):
        lanes = pl.ds(pl.multiple_of(base + block * LANES, LANES), LANES)
        x, y, z, fx, fy, fz, gx, gy, gz = [
            jnp.broadcast_to(scaled[k : k + 1, lanes], (SUBLANES, LANES)) for k in range(9)
        ]
        dx, dy, dz = point[0] - x, point[1] - y, point[2] - z
        square = dx * dx + dy * dy + dz * dz
        inverse = lax.rsqrt(jnp.maximum(square, SMALLEST))
        held = jnp.minimum(inverse, TOUCH_INVERSE)
        held_sq = held * held
        iso = jnp.maximum(held * (held_sq + 2.0), NEAR - square * inverse)
        along = dx * gx + dy * gy + dz * gz
        dyad = (inverse * (held_sq * (2.0 / 3.0 - held_sq))) * along
        terms = (iso * fx + dyad * dx, iso * fy + dyad * dy, iso * fz + dyad * dz)
        return terms if sums is None else tuple(one + term for one, term in zip(sums, terms))

    def tile_step(step, unused):
        first = pl.multiple_of(step * LANES, LANES)
        if beside is not None:
            beside(first)
        for group in range(LANES // SUBLANES):
            rows = pl.ds(first + group * SUBLANES, SUBLANES)
            point = [points_ref[k, rows, :] for k in range(3)]
            sums = None
            if before_ref is not None:
                sums = tuple(before_ref[k, rows, :] for k in range(3))
            if blocks == together:
                for block in range(together):
                    sums = add_block(point, 0, block, sums)
            else:

                def source_step(number, sums):
                    for block in range(together):
                        sums = add_block(point, number * (together * LANES), block, sums)
                    return sums

                zero = jnp.zeros((SUBLANES, LANES), jnp.float32)
                sums = lax.fori_loop(
                    0, blocks // together, source_step, sums or (zero, zero, zero)
                )
            for k in range(3):
                total_ref[k, pl.ds(first + shift + group * SUBLANES, SUBLANES), :] = sums[k]
        return unused

    lax.fori_loop(0, count // LANES, tile_step, 0)


def head_kernel(
    position_in,
    force_in,
    member_in,
    owner_in,
    source_ref,
    target_ref,
    owner_ref,
    position,
    force,
    member,
    arrived,
):
    moves = [(position_in, position), (force_in, force), (member_in, member), (owner_in, owner_ref)]
    copies = [
        pltpu.make_async_copy(there, here, arrived.at[number])
        for number, (there, here) in enumerate(moves)
    ]
    for copy in copies:
        copy.start()
    for copy in copies:
        copy.wait()
    source_ref[0:3, :] = position[...]
    source_ref[3:6, :] = force[...]
    target_ref[0:3, :] = position[...]
    target_ref[3:4, :] = member[...].astype(jnp.float32)


def place_targets(offset, target_ref, owner_ref, points_ref, match_ref):
    count = target_ref.shape[1]
    parts, rest = [], SCALE * target_ref[0:3, :]
    for _ in range(3):
        part = rest.astype(jnp.bfloat16).astype(jnp.float32)
        rest = rest - part
        parts.append(part)
    parts.append(jnp.zeros((7, count), jnp.float32))
    row = lax.broadcasted_iota(jnp.int32, (16, 3 * LANES), 0)
    lane = lax.broadcasted_iota(jnp.int32, (16, 3 * LANES), 1)
    chosen = jnp.where((row % 3 == lane // LANES) & (row < 9), 1.0, 0.0)
    points = lax.dot_general(
        jnp.concatenate(parts, axis=0).astype(jnp.bfloat16),
        chosen.astype(jnp.bfloat16),
        (((0,), (0,)), ((), ())),
        preferred_element_type=jnp.float32,
    )
    for k in range(3):
        points_ref[k, offset : offset + count, :] = points[:, k * LANES : (k + 1) * LANES]
    aggregates = match_ref.shape[0]
    labels = lax.broadcasted_iota(jnp.int32, (aggregates, count), 0)
    member = jnp.where(labels == target_ref[3:4, :].astype(jnp.int32), 1.0, 0.0)
    columns = lax.broadcasted_iota(jnp.int32, (aggregates, aggregates), 0)
    owner = jnp.where(columns == owner_ref[...], 1.0, 0.0)
    match_ref[:, offset : offset + count] = jnp.dot(
        owner.astype(jnp.bfloat16),
        member.astype(jnp.bfloat16),
        preferred_element_type=jnp.float32,
    ).astype(jnp.bfloat16)


def first_kernel(early, target_ref, source_ref, owner_ref, *refs):
    points_ref, total_ref, match_ref, scaled = refs[-4:]
    near = pl.ds(0, target_ref.shape[1])
    axis = SOURCE_AXES[0]
    first_half = 2 * lax.axis_index(axis) < lax.axis_size(axis)

    @pl.when(first_half if early else jnp.logical_not(first_half))
    def _():
        place_targets(0, target_ref, owner_ref, points_ref, match_ref)
        add_pairs(points_ref.at[:, near, :], source_ref, None, total_ref.at[:, near, :], scaled)


def middle_kernel(count, target_ref, source_ref, owner_ref, *refs):
    points_ref, total_ref, match_ref, scaled = refs[-4:]
    half, sources = target_ref.shape[1], source_ref.shape[1]
    near, far, rest = pl.ds(0, half), pl.ds(half, half), sources - count
    some = total_ref.at[:, near, :]
    if rest:
        add_pairs(
            points_ref.at[:, near, :],
            source_ref.at[:, pl.ds(count, rest)],
            some,
            some,
            scaled.at[:, pl.ds(0, rest)],
        )
    place_targets(half, target_ref, owner_ref, points_ref, match_ref)
    add_pairs(points_ref.at[:, far, :], source_ref, None, total_ref.at[:, far, :], scaled)


def last_kernel(
    unit_count,
    points_ref,
    source_ref,
    before_ref,
    match_ref,
    target_ref,
    keep_ref,
    send_ref,
    total,
    scaled,
    summed,
):
    count = target_ref.shape[1]
    tiles = count // LANES

    def sum_tile(first, tile):
        rows = pl.ds(first, LANES)
        for k in range(3):
            summed[tile, k : k + 1, :] = jnp.sum(total[k, rows, :].T, axis=0, keepdims=True)

    total[:, 0:LANES, :] = jnp.zeros((3, LANES, LANES), jnp.float32)
    add_pairs(
        points_ref,
        source_ref,
        before_ref,
        total,
        scaled,
        lambda first: sum_tile(first, first // LANES),
        LANES,
    )
    sum_tile(count, tiles)

    aggregates = match_ref.shape[0]
    per_unit, units = unit_count // LANES, count // unit_count
    first_row, unit_rows = sum_rows(aggregates), velocity_rows(unit_count)
    keep_ref[...] = jnp.zeros_like(keep_ref)
    send_ref[...] = jnp.zeros_like(send_ref)
    u = []
    for k in range(3):
        parts = [summed[tile + 1, k : k + 1, :] for tile in range(tiles)]
        u.append(jnp.concatenate(parts, axis=1))
        for tile in range(tiles):
            unit, block = divmod(tile, per_unit)
            packed, unit = (keep_ref, unit) if unit < units // 2 else (send_ref, unit - units // 2)
            row = first_row + unit * unit_rows + k * per_unit + block
            packed[row : row + 1, :] = parts[tile]
    x = [target_ref[k : k + 1, :] for k in range(3)]
    moments = jnp.concatenate(
        u
        + [
            x[1] * u[2] - x[2] * u[1],
            x[2] * u[0] - x[0] * u[2],
            x[0] * u[1] - x[1] * u[0],
        ]
        + x
        + [jnp.ones((1, count), jnp.float32), jnp.zeros((SUM_ROWS - 10, count), jnp.float32)],
        axis=0,
    )
    parts, rest = [], moments
    for _ in range(3):
        part = rest.astype(jnp.bfloat16)
        rest = rest - part.astype(jnp.float32)
        parts.append(part)
    products = [
        lax.dot_general(
            part,
            match_ref[...],
            (((1,), (1,)), ((), ())),
            preferred_element_type=jnp.float32,
        )
        for part in parts
    ]
    sums = (products[2] + products[1]) + products[0]
    for chunk, start in enumerate(range(0, aggregates, LANES)):
        width = min(LANES, aggregates - start)
        for packed in (keep_ref, send_ref):
            packed[chunk * SUM_ROWS : (chunk + 1) * SUM_ROWS, 0:width] = sums[
                :, start : start + width
            ]


def velocity_kernel(packed_ref, out_ref):
    per_unit = out_ref.shape[1] // LANES
    for k in range(3):
        for block in range(per_unit):
            row = k * per_unit + block
            out_ref[k : k + 1, block * LANES : (block + 1) * LANES] = packed_ref[row : row + 1, :]


def rigid_kernel(sums_ref, out_ref):
    columns = out_ref.shape[0]
    first = lax.axis_index(AXES) * columns
    lane = lax.broadcasted_iota(jnp.int32, (SUM_ROWS, LANES), 1)
    for column in range(columns):
        wanted = first + column
        mine = jnp.zeros((SUM_ROWS, LANES), jnp.float32)
        for chunk in range(sums_ref.shape[0] // SUM_ROWS):
            sums = sums_ref[chunk * SUM_ROWS : (chunk + 1) * SUM_ROWS, :]
            mine = jnp.where(lane + chunk * LANES == wanted, sums, mine)
        mine = jnp.where(lane == wanted % LANES, mine, 0.0)
        mine = jnp.sum(mine, axis=1, keepdims=True)
        u = [mine[k : k + 1] for k in range(3)]
        moment = [mine[3 + k : 4 + k] for k in range(3)]
        centre = [mine[6 + k : 7 + k] / mine[9:10] for k in range(3)]
        torque = [
            moment[0] - (centre[1] * u[2] - centre[2] * u[1]),
            moment[1] - (centre[2] * u[0] - centre[0] * u[2]),
            moment[2] - (centre[0] * u[1] - centre[1] * u[0]),
        ]
        for row, value in enumerate(u + torque + centre):
            out_ref[column : column + 1, row : row + 1] = value


def sum_rows(aggregates):
    return SUM_ROWS * pl.cdiv(aggregates, LANES)


def velocity_rows(count):
    return SUBLANES * pl.cdiv(3 * (count // LANES), SUBLANES)


WHOLE = pl.BlockSpec(memory_space=pltpu.VMEM)


def call(
    kernel, shapes, arguments, pairs=0, scratch=(), specs=None, vmem=8 << 20, aliases={}
):
    return pl.pallas_call(
        kernel,
        out_shape=[jax.ShapeDtypeStruct(shape, dtype) for shape, dtype in shapes],
        in_specs=specs or [WHOLE] * len(arguments),
        out_specs=[WHOLE] * len(shapes),
        scratch_shapes=list(scratch),
        input_output_aliases=aliases,
        compiler_params=pltpu.CompilerParams(vmem_limit_bytes=vmem),
        cost_estimate=pl.CostEstimate(
            flops=40 * pairs + 1000, bytes_accessed=1000, transcendentals=pairs
        ),
    )(*arguments)


def doubling(mesh, axes):
    steps = []
    cores = mesh.shape["sub"]
    other = 1 if cores == 2 else 0
    for axis in axes:
        size = mesh.shape[axis]
        reach = 1
        while reach < size:
            if axis == "sub":
                steps.append((axis, [(i, i ^ reach) for i in range(size)]))
            else:
                flip = reach * cores + other
                steps.append(((axis, "sub"), [(i, i ^ flip) for i in range(size * cores)]))
            reach *= 2
    return steps


def on_device(source_steps, target_steps, devices, positions, forces, membership, owner_slot):
    count, aggregates = positions.shape[1], owner_slot.shape[0]
    real = jnp.float32
    sources, targets, owner = call(
        head_kernel,
        [((6, count), real), ((4, count), real), ((1, aggregates), jnp.int32)],
        [
            pltpu.with_memory_space_constraint(one, pltpu.HBM)
            for one in (positions, forces, membership[None, :], owner_slot[None, :])
        ],
        scratch=[
            pltpu.VMEM((3, count), real),
            pltpu.VMEM((3, count), real),
            pltpu.VMEM((1, count), jnp.int32),
            pltpu.SemaphoreType.DMA((4,)),
        ],
        specs=[pl.BlockSpec(memory_space=pltpu.HBM)] * 4,
    )

    arriving = coming = None
    own = sources
    for number in range(max(len(source_steps) - 1, len(target_steps))):
        if number < len(target_steps):
            if number:
                targets = jnp.concatenate([targets, arriving], axis=1)
            axis, pairs = target_steps[number]
            arriving = lax.ppermute(targets, axis, pairs)
        if number < len(source_steps) - 1:
            if number:
                sources = jnp.concatenate([sources, coming], axis=1)
            axis, pairs = source_steps[number]
            coming = lax.ppermute(sources, axis, pairs)
    half = targets.shape[1]
    seen = 2 * half
    vmem = (8 << 20) + 4 * (4 * 3 * seen * LANES)
    shapes = [
        ((3, seen, LANES), real),
        ((3, seen, LANES), real),
        ((aggregates, seen), jnp.bfloat16),
    ]

    def scaled(width):
        return pltpu.VMEM((2 * SUBLANES, width), real)

    filled = call(
        functools.partial(first_kernel, True),
        shapes,
        (targets, own, owner),
        pairs=half * count,
        scratch=[scaled(count)],
        vmem=vmem,
    )
    if coming is not None:
        *filled, coming = lax.optimization_barrier((*filled, coming))
        sources = jnp.concatenate([sources, coming], axis=1)
    axis, pairs = source_steps[-1]
    coming = lax.ppermute(sources, axis, pairs)
    filled = call(
        functools.partial(first_kernel, False),
        shapes,
        (targets, own, owner, *filled),
        pairs=half * count,
        scratch=[scaled(count)],
        vmem=vmem,
        aliases={3: 0, 4: 1, 5: 2},
    )
    *filled, arriving = lax.optimization_barrier((*filled, arriving))
    points, total, match = call(
        functools.partial(middle_kernel, count),
        shapes,
        (arriving, sources, owner, *filled),
        pairs=seen * sources.shape[1] - half * count,
        scratch=[scaled(sources.shape[1])],
        vmem=vmem,
        aliases={3: 0, 4: 1, 5: 2},
    )
    targets = jnp.concatenate([targets, arriving], axis=1)
    total, coming = lax.optimization_barrier((total, coming))
    first_row, units = sum_rows(aggregates), seen // count
    unit_rows = velocity_rows(count)
    packed = ((first_row + units // 2 * unit_rows, LANES), real)
    keep, send = call(
        functools.partial(last_kernel, count),
        [packed, packed],
        (points, coming, total, match, targets),
        pairs=seen * coming.shape[1],
        scratch=[
            pltpu.VMEM((3, seen + LANES, LANES), real),
            scaled(sources.shape[1]),
            pltpu.VMEM((seen // LANES + 1, SUBLANES, LANES), real),
        ],
        vmem=vmem,
    )

    for axis, pairs in reversed(target_steps):
        if keep is None:
            half = (both.shape[0] - first_row) // 2
            keep = both[: first_row + half]
            send = jnp.concatenate([both[:first_row], both[first_row + half :]], axis=0)
        both = keep + lax.ppermute(send, axis, pairs)
        keep = None
    sums, mine = both[:first_row], both[first_row:]
    for number, (axis, pairs) in enumerate(source_steps):
        coming = lax.ppermute(sums, axis, pairs)
        if number == 0:
            (velocity,) = call(velocity_kernel, [((3, count), real)], (mine,))
            velocity, coming = lax.optimization_barrier((velocity, coming))
        sums = sums + coming
    columns = aggregates // devices
    (rigid,) = call(rigid_kernel, [((columns, 9), real)], (sums,))
    return velocity, rigid.T


def solution(mesh):
    placed = (
        P(None, ("groups",) + AXES),
        P(None, ("groups",) + AXES),
        P(("groups",) + AXES),
        P("groups"),
    )
    devices = math.prod(mesh.shape[axis] for axis in AXES)
    return jax.shard_map(
        functools.partial(
            on_device, doubling(mesh, SOURCE_AXES), doubling(mesh, TARGET_AXES), devices
        ),
        mesh=mesh,
        in_specs=placed,
        out_specs=(P(None, ("groups",) + AXES), P(None, ("groups",) + AXES)),
        check_vma=False,
    )
```

```python
import functools
import math

import jax
import jax.numpy as jnp
from jax import lax
from jax.experimental import pallas as pl
from jax.experimental.pallas import tpu as pltpu
from jax.sharding import PartitionSpec as P

SCALE = math.sqrt(0.75)
ISO = 9.0 / (32.0 * SCALE)
DYAD = 3.0 * ISO
NEAR = 1.0 / ISO
TOUCH_INVERSE = 1.0 / (2.0 * SCALE)
SMALLEST = 1.1754944e-38

LANES = 128
SUBLANES = 8
BLOCKS_AT_ONCE = 4
SUM_ROWS = 16
SOURCE_AXES = ("tgt",)
TARGET_AXES = ("sub", "src")
AXES = ("tgt", "src", "sub")


def add_pairs(
    points_ref, source_ref, before_ref, total_ref, scaled, beside=None, shift=0, unrolled=1
):
    count = total_ref.shape[1] - shift
    blocks = source_ref.shape[1] // LANES
    together = math.gcd(blocks, BLOCKS_AT_ONCE)
    scaled[0:3, :] = SCALE * source_ref[0:3, :]
    scaled[3:6, :] = ISO * source_ref[3:6, :]
    scaled[6:9, :] = DYAD * source_ref[3:6, :]

    def add_block(point, base, block, sums):
        lanes = pl.ds(pl.multiple_of(base + block * LANES, LANES), LANES)
        x, y, z, fx, fy, fz, gx, gy, gz = [
            jnp.broadcast_to(scaled[k : k + 1, lanes], (SUBLANES, LANES)) for k in range(9)
        ]
        dx, dy, dz = point[0] - x, point[1] - y, point[2] - z
        square = dx * dx + dy * dy + dz * dz
        inverse = lax.rsqrt(jnp.maximum(square, SMALLEST))
        held = jnp.minimum(inverse, TOUCH_INVERSE)
        held_sq = held * held
        iso = jnp.maximum(held * (held_sq + 2.0), NEAR - square * inverse)
        along = dx * gx + dy * gy + dz * gz
        dyad = (inverse * (held_sq * (2.0 / 3.0 - held_sq))) * along
        terms = (iso * fx + dyad * dx, iso * fy + dyad * dy, iso * fz + dyad * dz)
        return terms if sums is None else tuple(one + term for one, term in zip(sums, terms))

    def tile_step(step, unused):
        first = step * LANES if isinstance(step, int) else pl.multiple_of(step * LANES, LANES)
        if beside is not None:
            beside(first)
        for group in range(LANES // SUBLANES):
            rows = pl.ds(first + group * SUBLANES, SUBLANES)
            point = [points_ref[k, rows, :] for k in range(3)]
            sums = None
            if before_ref is not None:
                sums = tuple(before_ref[k, rows, :] for k in range(3))
            if blocks == together:
                for block in range(together):
                    sums = add_block(point, 0, block, sums)
            else:

                def source_step(number, sums):
                    for block in range(together):
                        sums = add_block(point, number * (together * LANES), block, sums)
                    return sums

                zero = jnp.zeros((SUBLANES, LANES), jnp.float32)
                sums = lax.fori_loop(
                    0, blocks // together, source_step, sums or (zero, zero, zero)
                )
            for k in range(3):
                total_ref[k, pl.ds(first + shift + group * SUBLANES, SUBLANES), :] = sums[k]
        return unused

    tiles = count // LANES
    if tiles <= unrolled:
        for tile in range(tiles):
            tile_step(tile, 0)
    else:
        lax.fori_loop(0, tiles, tile_step, 0)


def head_kernel(
    position_in,
    force_in,
    member_in,
    owner_in,
    source_ref,
    target_ref,
    owner_ref,
    position,
    force,
    member,
    arrived,
):
    moves = [(position_in, position), (force_in, force), (member_in, member), (owner_in, owner_ref)]
    copies = [
        pltpu.make_async_copy(there, here, arrived.at[number])
        for number, (there, here) in enumerate(moves)
    ]
    for copy in copies:
        copy.start()
    for copy in copies:
        copy.wait()
    source_ref[0:3, :] = position[...]
    source_ref[3:6, :] = force[...]
    target_ref[0:3, :] = position[...]
    target_ref[3:4, :] = member[...].astype(jnp.float32)


def place_targets(offset, target_ref, owner_ref, points_ref, match_ref):
    count = target_ref.shape[1]
    parts, rest = [], SCALE * target_ref[0:3, :]
    for _ in range(3):
        part = rest.astype(jnp.bfloat16).astype(jnp.float32)
        rest = rest - part
        parts.append(part)
    parts.append(jnp.zeros((7, count), jnp.float32))
    row = lax.broadcasted_iota(jnp.int32, (16, 3 * LANES), 0)
    lane = lax.broadcasted_iota(jnp.int32, (16, 3 * LANES), 1)
    chosen = jnp.where((row % 3 == lane // LANES) & (row < 9), 1.0, 0.0)
    points = lax.dot_general(
        jnp.concatenate(parts, axis=0).astype(jnp.bfloat16),
        chosen.astype(jnp.bfloat16),
        (((0,), (0,)), ((), ())),
        preferred_element_type=jnp.float32,
    )
    for k in range(3):
        points_ref[k, offset : offset + count, :] = points[:, k * LANES : (k + 1) * LANES]
    aggregates = match_ref.shape[0]
    labels = lax.broadcasted_iota(jnp.int32, (aggregates, count), 0)
    member = jnp.where(labels == target_ref[3:4, :].astype(jnp.int32), 1.0, 0.0)
    columns = lax.broadcasted_iota(jnp.int32, (aggregates, aggregates), 0)
    owner = jnp.where(columns == owner_ref[...], 1.0, 0.0)
    match_ref[:, offset : offset + count] = jnp.dot(
        owner.astype(jnp.bfloat16),
        member.astype(jnp.bfloat16),
        preferred_element_type=jnp.float32,
    ).astype(jnp.bfloat16)


def first_kernel(early, target_ref, source_ref, owner_ref, *refs):
    points_ref, total_ref, match_ref, scaled = refs[-4:]
    near = pl.ds(0, target_ref.shape[1])
    axis = SOURCE_AXES[0]
    first_half = 2 * lax.axis_index(axis) < lax.axis_size(axis)

    @pl.when(first_half if early else jnp.logical_not(first_half))
    def _():
        place_targets(0, target_ref, owner_ref, points_ref, match_ref)
        add_pairs(
            points_ref.at[:, near, :],
            source_ref,
            None,
            total_ref.at[:, near, :],
            scaled,
            unrolled=4,
        )


def middle_kernel(count, target_ref, source_ref, owner_ref, *refs):
    points_ref, total_ref, match_ref, scaled = refs[-4:]
    half, sources = target_ref.shape[1], source_ref.shape[1]
    near, far, rest = pl.ds(0, half), pl.ds(half, half), sources - count
    some = total_ref.at[:, near, :]
    place_targets(half, target_ref, owner_ref, points_ref, match_ref)
    if rest:
        add_pairs(
            points_ref.at[:, near, :],
            source_ref.at[:, pl.ds(count, rest)],
            some,
            some,
            scaled.at[:, pl.ds(0, rest)],
            unrolled=4,
        )
    add_pairs(points_ref.at[:, far, :], source_ref, None, total_ref.at[:, far, :], scaled)


def last_kernel(
    unit_count,
    points_ref,
    source_ref,
    before_ref,
    match_ref,
    target_ref,
    keep_ref,
    send_ref,
    total,
    scaled,
    summed,
):
    count = target_ref.shape[1]
    tiles = count // LANES

    def sum_tile(first, tile):
        rows = pl.ds(first, LANES)
        for k in range(3):
            summed[tile, k : k + 1, :] = jnp.sum(total[k, rows, :].T, axis=0, keepdims=True)

    total[:, 0:LANES, :] = jnp.zeros((3, LANES, LANES), jnp.float32)
    add_pairs(
        points_ref,
        source_ref,
        before_ref,
        total,
        scaled,
        lambda first: sum_tile(first, first // LANES),
        LANES,
    )
    sum_tile(count, tiles)

    aggregates = match_ref.shape[0]
    per_unit, units = unit_count // LANES, count // unit_count
    first_row, unit_rows = sum_rows(aggregates), velocity_rows(unit_count)
    keep_ref[...] = jnp.zeros_like(keep_ref)
    send_ref[...] = jnp.zeros_like(send_ref)
    u = []
    for k in range(3):
        parts = [summed[tile + 1, k : k + 1, :] for tile in range(tiles)]
        u.append(jnp.concatenate(parts, axis=1))
        for tile in range(tiles):
            unit, block = divmod(tile, per_unit)
            packed, unit = (keep_ref, unit) if unit < units // 2 else (send_ref, unit - units // 2)
            row = first_row + unit * unit_rows + k * per_unit + block
            packed[row : row + 1, :] = parts[tile]
    x = [target_ref[k : k + 1, :] for k in range(3)]
    moments = jnp.concatenate(
        u
        + [
            x[1] * u[2] - x[2] * u[1],
            x[2] * u[0] - x[0] * u[2],
            x[0] * u[1] - x[1] * u[0],
        ]
        + x
        + [jnp.ones((1, count), jnp.float32), jnp.zeros((SUM_ROWS - 10, count), jnp.float32)],
        axis=0,
    )
    parts, rest = [], moments
    for _ in range(3):
        part = rest.astype(jnp.bfloat16)
        rest = rest - part.astype(jnp.float32)
        parts.append(part)
    products = [
        lax.dot_general(
            part,
            match_ref[...],
            (((1,), (1,)), ((), ())),
            preferred_element_type=jnp.float32,
        )
        for part in parts
    ]
    sums = (products[2] + products[1]) + products[0]
    for chunk, start in enumerate(range(0, aggregates, LANES)):
        width = min(LANES, aggregates - start)
        for packed in (keep_ref, send_ref):
            packed[chunk * SUM_ROWS : (chunk + 1) * SUM_ROWS, 0:width] = sums[
                :, start : start + width
            ]


def velocity_kernel(packed_ref, out_ref):
    per_unit = out_ref.shape[1] // LANES
    for k in range(3):
        for block in range(per_unit):
            row = k * per_unit + block
            out_ref[k : k + 1, block * LANES : (block + 1) * LANES] = packed_ref[row : row + 1, :]


def rigid_kernel(sums_ref, out_ref):
    columns = out_ref.shape[0]
    first = lax.axis_index(AXES) * columns
    lane = lax.broadcasted_iota(jnp.int32, (SUM_ROWS, LANES), 1)
    for column in range(columns):
        wanted = first + column
        mine = jnp.zeros((SUM_ROWS, LANES), jnp.float32)
        for chunk in range(sums_ref.shape[0] // SUM_ROWS):
            sums = sums_ref[chunk * SUM_ROWS : (chunk + 1) * SUM_ROWS, :]
            mine = jnp.where(lane + chunk * LANES == wanted, sums, mine)
        mine = jnp.where(lane == wanted % LANES, mine, 0.0)
        mine = jnp.sum(mine, axis=1, keepdims=True)
        u = [mine[k : k + 1] for k in range(3)]
        moment = [mine[3 + k : 4 + k] for k in range(3)]
        centre = [mine[6 + k : 7 + k] / mine[9:10] for k in range(3)]
        torque = [
            moment[0] - (centre[1] * u[2] - centre[2] * u[1]),
            moment[1] - (centre[2] * u[0] - centre[0] * u[2]),
            moment[2] - (centre[0] * u[1] - centre[1] * u[0]),
        ]
        for row, value in enumerate(u + torque + centre):
            out_ref[column : column + 1, row : row + 1] = value


def sum_rows(aggregates):
    return SUM_ROWS * pl.cdiv(aggregates, LANES)


def velocity_rows(count):
    return SUBLANES * pl.cdiv(3 * (count // LANES), SUBLANES)


WHOLE = pl.BlockSpec(memory_space=pltpu.VMEM)


def call(
    kernel, shapes, arguments, pairs=0, scratch=(), specs=None, vmem=8 << 20, aliases={}
):
    return pl.pallas_call(
        kernel,
        out_shape=[jax.ShapeDtypeStruct(shape, dtype) for shape, dtype in shapes],
        in_specs=specs or [WHOLE] * len(arguments),
        out_specs=[WHOLE] * len(shapes),
        scratch_shapes=list(scratch),
        input_output_aliases=aliases,
        compiler_params=pltpu.CompilerParams(vmem_limit_bytes=vmem),
        cost_estimate=pl.CostEstimate(
            flops=40 * pairs + 1000, bytes_accessed=1000, transcendentals=pairs
        ),
    )(*arguments)


def doubling(mesh, axes):
    steps = []
    cores = mesh.shape["sub"]
    other = 1 if cores == 2 else 0
    for axis in axes:
        size = mesh.shape[axis]
        reach = 1
        while reach < size:
            if axis == "sub":
                steps.append((axis, [(i, i ^ reach) for i in range(size)]))
            else:
                flip = reach * cores + other
                steps.append(((axis, "sub"), [(i, i ^ flip) for i in range(size * cores)]))
            reach *= 2
    return steps


def on_device(source_steps, target_steps, devices, positions, forces, membership, owner_slot):
    count, aggregates = positions.shape[1], owner_slot.shape[0]
    real = jnp.float32
    sources, targets, owner = call(
        head_kernel,
        [((6, count), real), ((4, count), real), ((1, aggregates), jnp.int32)],
        [
            pltpu.with_memory_space_constraint(one, pltpu.HBM)
            for one in (positions, forces, membership[None, :], owner_slot[None, :])
        ],
        scratch=[
            pltpu.VMEM((3, count), real),
            pltpu.VMEM((3, count), real),
            pltpu.VMEM((1, count), jnp.int32),
            pltpu.SemaphoreType.DMA((4,)),
        ],
        specs=[pl.BlockSpec(memory_space=pltpu.HBM)] * 4,
    )

    arriving = coming = None
    own = sources
    for number in range(max(len(source_steps) - 1, len(target_steps))):
        if number < len(target_steps):
            if number:
                targets = jnp.concatenate([targets, arriving], axis=1)
            axis, pairs = target_steps[number]
            arriving = lax.ppermute(targets, axis, pairs)
        if number < len(source_steps) - 1:
            if number:
                sources = jnp.concatenate([sources, coming], axis=1)
            axis, pairs = source_steps[number]
            coming = lax.ppermute(sources, axis, pairs)
    half = targets.shape[1]
    seen = 2 * half
    vmem = (8 << 20) + 4 * (4 * 3 * seen * LANES)
    shapes = [
        ((3, seen, LANES), real),
        ((3, seen, LANES), real),
        ((aggregates, seen), jnp.bfloat16),
    ]

    def scaled(width):
        return pltpu.VMEM((2 * SUBLANES, width), real)

    filled = call(
        functools.partial(first_kernel, True),
        shapes,
        (targets, own, owner),
        pairs=half * count,
        scratch=[scaled(count)],
        vmem=vmem,
    )
    if coming is not None:
        *filled, coming = lax.optimization_barrier((*filled, coming))
        sources = jnp.concatenate([sources, coming], axis=1)
    axis, pairs = source_steps[-1]
    coming = lax.ppermute(sources, axis, pairs)
    filled = call(
        functools.partial(first_kernel, False),
        shapes,
        (targets, own, owner, *filled),
        pairs=half * count,
        scratch=[scaled(count)],
        vmem=vmem,
        aliases={3: 0, 4: 1, 5: 2},
    )
    *filled, arriving = lax.optimization_barrier((*filled, arriving))
    points, total, match = call(
        functools.partial(middle_kernel, count),
        shapes,
        (arriving, sources, owner, *filled),
        pairs=seen * sources.shape[1] - half * count,
        scratch=[scaled(sources.shape[1])],
        vmem=vmem,
        aliases={3: 0, 4: 1, 5: 2},
    )
    targets = jnp.concatenate([targets, arriving], axis=1)
    total, coming = lax.optimization_barrier((total, coming))
    first_row, units = sum_rows(aggregates), seen // count
    unit_rows = velocity_rows(count)
    packed = ((first_row + units // 2 * unit_rows, LANES), real)
    keep, send = call(
        functools.partial(last_kernel, count),
        [packed, packed],
        (points, coming, total, match, targets),
        pairs=seen * coming.shape[1],
        scratch=[
            pltpu.VMEM((3, seen + LANES, LANES), real),
            scaled(sources.shape[1]),
            pltpu.VMEM((seen // LANES + 1, SUBLANES, LANES), real),
        ],
        vmem=vmem,
    )

    for axis, pairs in reversed(target_steps):
        if keep is None:
            half = (both.shape[0] - first_row) // 2
            keep = both[: first_row + half]
            send = jnp.concatenate([both[:first_row], both[first_row + half :]], axis=0)
        both = keep + lax.ppermute(send, axis, pairs)
        keep = None
    sums, mine = both[:first_row], both[first_row:]
    for number, (axis, pairs) in enumerate(source_steps):
        coming = lax.ppermute(sums, axis, pairs)
        if number == 0:
            (velocity,) = call(velocity_kernel, [((3, count), real)], (mine,))
            velocity, coming = lax.optimization_barrier((velocity, coming))
        sums = sums + coming
    columns = aggregates // devices
    (rigid,) = call(rigid_kernel, [((columns, 9), real)], (sums,))
    return velocity, rigid.T


def solution(mesh):
    placed = (
        P(None, ("groups",) + AXES),
        P(None, ("groups",) + AXES),
        P(("groups",) + AXES),
        P("groups"),
    )
    devices = math.prod(mesh.shape[axis] for axis in AXES)
    return jax.shard_map(
        functools.partial(
            on_device, doubling(mesh, SOURCE_AXES), doubling(mesh, TARGET_AXES), devices
        ),
        mesh=mesh,
        in_specs=placed,
        out_specs=(P(None, ("groups",) + AXES), P(None, ("groups",) + AXES)),
        check_vma=False,
    )
```

```python
import functools
import math

import jax
import jax.numpy as jnp
from jax import lax
from jax.experimental import pallas as pl
from jax.experimental.pallas import tpu as pltpu
from jax.sharding import PartitionSpec as P

SCALE = math.sqrt(0.75)
ISO = 9.0 / (32.0 * SCALE)
DYAD = 3.0 * ISO
NEAR = 1.0 / ISO
TOUCH_INVERSE = 1.0 / (2.0 * SCALE)
SMALLEST = 1.1754944e-38

LANES = 128
SUBLANES = 8
BLOCKS_AT_ONCE = 4
SUM_ROWS = 16
SOURCE_AXES = ("tgt",)
TARGET_AXES = ("sub", "src")
AXES = ("tgt", "src", "sub")


def add_pairs(
    points_ref, source_ref, before_ref, total_ref, scaled, beside=None, shift=0, unrolled=1
):
    count = total_ref.shape[1] - shift
    blocks = source_ref.shape[1] // LANES
    together = math.gcd(blocks, BLOCKS_AT_ONCE)
    scaled[0:3, :] = SCALE * source_ref[0:3, :]
    scaled[3:6, :] = ISO * source_ref[3:6, :]
    scaled[6:9, :] = DYAD * source_ref[3:6, :]

    def add_block(point, base, block, sums):
        lanes = pl.ds(pl.multiple_of(base + block * LANES, LANES), LANES)
        x, y, z, fx, fy, fz, gx, gy, gz = [
            jnp.broadcast_to(scaled[k : k + 1, lanes], (SUBLANES, LANES)) for k in range(9)
        ]
        dx, dy, dz = point[0] - x, point[1] - y, point[2] - z
        square = dx * dx + dy * dy + dz * dz
        inverse = lax.rsqrt(jnp.maximum(square, SMALLEST))
        held = jnp.minimum(inverse, TOUCH_INVERSE)
        held_sq = held * held
        iso = jnp.maximum(held * (held_sq + 2.0), NEAR - square * inverse)
        along = dx * gx + dy * gy + dz * gz
        dyad = (inverse * (held_sq * (2.0 / 3.0 - held_sq))) * along
        terms = (iso * fx + dyad * dx, iso * fy + dyad * dy, iso * fz + dyad * dz)
        return terms if sums is None else tuple(one + term for one, term in zip(sums, terms))

    def tile_step(step, unused):
        first = step * LANES if isinstance(step, int) else pl.multiple_of(step * LANES, LANES)
        if beside is not None:
            beside(first)
        for group in range(LANES // SUBLANES):
            rows = pl.ds(first + group * SUBLANES, SUBLANES)
            point = [points_ref[k, rows, :] for k in range(3)]
            sums = None
            if before_ref is not None:
                sums = tuple(before_ref[k, rows, :] for k in range(3))
            if blocks == together:
                for block in range(together):
                    sums = add_block(point, 0, block, sums)
            else:

                def source_step(number, sums):
                    for block in range(together):
                        sums = add_block(point, number * (together * LANES), block, sums)
                    return sums

                zero = jnp.zeros((SUBLANES, LANES), jnp.float32)
                sums = lax.fori_loop(
                    0, blocks // together, source_step, sums or (zero, zero, zero)
                )
            for k in range(3):
                total_ref[k, pl.ds(first + shift + group * SUBLANES, SUBLANES), :] = sums[k]
        return unused

    tiles = count // LANES
    if tiles <= unrolled:
        for tile in range(tiles):
            tile_step(tile, 0)
    else:
        lax.fori_loop(0, tiles, tile_step, 0, unroll=2 if tiles % 2 == 0 else 1)


def head_kernel(
    position_in,
    force_in,
    member_in,
    owner_in,
    source_ref,
    target_ref,
    owner_ref,
    position,
    force,
    member,
    arrived,
):
    moves = [(position_in, position), (force_in, force), (member_in, member), (owner_in, owner_ref)]
    copies = [
        pltpu.make_async_copy(there, here, arrived.at[number])
        for number, (there, here) in enumerate(moves)
    ]
    for copy in copies:
        copy.start()
    for copy in copies:
        copy.wait()
    source_ref[0:3, :] = position[...]
    source_ref[3:6, :] = force[...]
    target_ref[0:3, :] = position[...]
    target_ref[3:4, :] = member[...].astype(jnp.float32)


def place_targets(offset, target_ref, owner_ref, points_ref, match_ref):
    count = target_ref.shape[1]
    parts, rest = [], SCALE * target_ref[0:3, :]
    for _ in range(3):
        part = rest.astype(jnp.bfloat16).astype(jnp.float32)
        rest = rest - part
        parts.append(part)
    parts.append(jnp.zeros((7, count), jnp.float32))
    row = lax.broadcasted_iota(jnp.int32, (16, 3 * LANES), 0)
    lane = lax.broadcasted_iota(jnp.int32, (16, 3 * LANES), 1)
    chosen = jnp.where((row % 3 == lane // LANES) & (row < 9), 1.0, 0.0)
    stacked = jnp.concatenate(parts, axis=0).astype(jnp.bfloat16)
    for start in range(0, count, LANES):
        points = lax.dot_general(
            stacked[:, start : start + LANES],
            chosen.astype(jnp.bfloat16),
            (((0,), (0,)), ((), ())),
            preferred_element_type=jnp.float32,
        )
        rows = slice(offset + start, offset + start + LANES)
        for k in range(3):
            points_ref[k, rows, :] = points[:, k * LANES : (k + 1) * LANES]
    aggregates = match_ref.shape[0]
    labels = lax.broadcasted_iota(jnp.int32, (aggregates, count), 0)
    member = jnp.where(labels == target_ref[3:4, :].astype(jnp.int32), 1.0, 0.0)
    columns = lax.broadcasted_iota(jnp.int32, (aggregates, aggregates), 0)
    owner = jnp.where(columns == owner_ref[...], 1.0, 0.0)
    match_ref[:, offset : offset + count] = jnp.dot(
        owner.astype(jnp.bfloat16),
        member.astype(jnp.bfloat16),
        preferred_element_type=jnp.float32,
    ).astype(jnp.bfloat16)


def first_kernel(early, target_ref, source_ref, owner_ref, *refs):
    points_ref, total_ref, match_ref, scaled = refs[-4:]
    near = pl.ds(0, target_ref.shape[1])
    axis = SOURCE_AXES[0]
    first_half = 2 * lax.axis_index(axis) < lax.axis_size(axis)

    @pl.when(first_half if early else jnp.logical_not(first_half))
    def _():
        place_targets(0, target_ref, owner_ref, points_ref, match_ref)
        add_pairs(
            points_ref.at[:, near, :],
            source_ref,
            None,
            total_ref.at[:, near, :],
            scaled,
            unrolled=4,
        )


def middle_kernel(count, target_ref, source_ref, owner_ref, *refs):
    points_ref, total_ref, match_ref, scaled = refs[-4:]
    half, sources = target_ref.shape[1], source_ref.shape[1]
    near, far, rest = pl.ds(0, half), pl.ds(half, half), sources - count
    some = total_ref.at[:, near, :]
    place_targets(half, target_ref, owner_ref, points_ref, match_ref)
    if rest:
        add_pairs(
            points_ref.at[:, near, :],
            source_ref.at[:, pl.ds(count, rest)],
            some,
            some,
            scaled.at[:, pl.ds(0, rest)],
            unrolled=4,
        )
    add_pairs(points_ref.at[:, far, :], source_ref, None, total_ref.at[:, far, :], scaled)


def last_kernel(
    unit_count,
    points_ref,
    source_ref,
    before_ref,
    match_ref,
    target_ref,
    keep_ref,
    send_ref,
    total,
    scaled,
    summed,
):
    count = target_ref.shape[1]
    tiles = count // LANES

    def sum_tile(first, tile):
        rows = pl.ds(first, LANES)
        for k in range(3):
            summed[tile, k : k + 1, :] = jnp.sum(total[k, rows, :].T, axis=0, keepdims=True)

    total[:, 0:LANES, :] = jnp.zeros((3, LANES, LANES), jnp.float32)
    add_pairs(
        points_ref,
        source_ref,
        before_ref,
        total,
        scaled,
        lambda first: sum_tile(first, first // LANES),
        LANES,
    )
    sum_tile(count, tiles)

    aggregates = match_ref.shape[0]
    per_unit, units = unit_count // LANES, count // unit_count
    first_row, unit_rows = sum_rows(aggregates), velocity_rows(unit_count)
    keep_ref[...] = jnp.zeros_like(keep_ref)
    send_ref[...] = jnp.zeros_like(send_ref)
    u = []
    for k in range(3):
        parts = [summed[tile + 1, k : k + 1, :] for tile in range(tiles)]
        u.append(jnp.concatenate(parts, axis=1))
        for tile in range(tiles):
            unit, block = divmod(tile, per_unit)
            packed, unit = (keep_ref, unit) if unit < units // 2 else (send_ref, unit - units // 2)
            row = first_row + unit * unit_rows + k * per_unit + block
            packed[row : row + 1, :] = parts[tile]
    x = [target_ref[k : k + 1, :] for k in range(3)]
    moments = jnp.concatenate(
        u
        + [
            x[1] * u[2] - x[2] * u[1],
            x[2] * u[0] - x[0] * u[2],
            x[0] * u[1] - x[1] * u[0],
        ]
        + x
        + [jnp.ones((1, count), jnp.float32), jnp.zeros((SUM_ROWS - 10, count), jnp.float32)],
        axis=0,
    )
    parts, rest = [], moments
    for _ in range(3):
        part = rest.astype(jnp.bfloat16)
        rest = rest - part.astype(jnp.float32)
        parts.append(part)
    products = [
        lax.dot_general(
            part,
            match_ref[...],
            (((1,), (1,)), ((), ())),
            preferred_element_type=jnp.float32,
        )
        for part in parts
    ]
    sums = (products[2] + products[1]) + products[0]
    for chunk, start in enumerate(range(0, aggregates, LANES)):
        width = min(LANES, aggregates - start)
        for packed in (keep_ref, send_ref):
            packed[chunk * SUM_ROWS : (chunk + 1) * SUM_ROWS, 0:width] = sums[
                :, start : start + width
            ]


def velocity_kernel(packed_ref, out_ref):
    per_unit = out_ref.shape[1] // LANES
    for k in range(3):
        for block in range(per_unit):
            row = k * per_unit + block
            out_ref[k : k + 1, block * LANES : (block + 1) * LANES] = packed_ref[row : row + 1, :]


def rigid_kernel(sums_ref, out_ref):
    columns = out_ref.shape[0]
    first = lax.axis_index(AXES) * columns
    lane = lax.broadcasted_iota(jnp.int32, (SUM_ROWS, LANES), 1)
    for column in range(columns):
        wanted = first + column
        mine = jnp.zeros((SUM_ROWS, LANES), jnp.float32)
        for chunk in range(sums_ref.shape[0] // SUM_ROWS):
            sums = sums_ref[chunk * SUM_ROWS : (chunk + 1) * SUM_ROWS, :]
            mine = jnp.where(lane + chunk * LANES == wanted, sums, mine)
        mine = jnp.where(lane == wanted % LANES, mine, 0.0)
        mine = jnp.sum(mine, axis=1, keepdims=True)
        u = [mine[k : k + 1] for k in range(3)]
        moment = [mine[3 + k : 4 + k] for k in range(3)]
        centre = [mine[6 + k : 7 + k] / mine[9:10] for k in range(3)]
        torque = [
            moment[0] - (centre[1] * u[2] - centre[2] * u[1]),
            moment[1] - (centre[2] * u[0] - centre[0] * u[2]),
            moment[2] - (centre[0] * u[1] - centre[1] * u[0]),
        ]
        for row, value in enumerate(u + torque + centre):
            out_ref[column : column + 1, row : row + 1] = value


def sum_rows(aggregates):
    return SUM_ROWS * pl.cdiv(aggregates, LANES)


def velocity_rows(count):
    return SUBLANES * pl.cdiv(3 * (count // LANES), SUBLANES)


WHOLE = pl.BlockSpec(memory_space=pltpu.VMEM)


def call(
    kernel, shapes, arguments, pairs=0, scratch=(), specs=None, vmem=8 << 20, aliases={}
):
    return pl.pallas_call(
        kernel,
        out_shape=[jax.ShapeDtypeStruct(shape, dtype) for shape, dtype in shapes],
        in_specs=specs or [WHOLE] * len(arguments),
        out_specs=[WHOLE] * len(shapes),
        scratch_shapes=list(scratch),
        input_output_aliases=aliases,
        compiler_params=pltpu.CompilerParams(vmem_limit_bytes=vmem),
        cost_estimate=pl.CostEstimate(
            flops=40 * pairs + 1000, bytes_accessed=1000, transcendentals=pairs
        ),
    )(*arguments)


def doubling(mesh, axes):
    steps = []
    cores = mesh.shape["sub"]
    other = 1 if cores == 2 else 0
    for axis in axes:
        size = mesh.shape[axis]
        reach = 1
        while reach < size:
            if axis == "sub":
                steps.append((axis, [(i, i ^ reach) for i in range(size)]))
            else:
                flip = reach * cores + other
                steps.append(((axis, "sub"), [(i, i ^ flip) for i in range(size * cores)]))
            reach *= 2
    return steps


def on_device(source_steps, target_steps, devices, positions, forces, membership, owner_slot):
    count, aggregates = positions.shape[1], owner_slot.shape[0]
    real = jnp.float32
    sources, targets, owner = call(
        head_kernel,
        [((6, count), real), ((4, count), real), ((1, aggregates), jnp.int32)],
        [
            pltpu.with_memory_space_constraint(one, pltpu.HBM)
            for one in (positions, forces, membership[None, :], owner_slot[None, :])
        ],
        scratch=[
            pltpu.VMEM((3, count), real),
            pltpu.VMEM((3, count), real),
            pltpu.VMEM((1, count), jnp.int32),
            pltpu.SemaphoreType.DMA((4,)),
        ],
        specs=[pl.BlockSpec(memory_space=pltpu.HBM)] * 4,
    )

    arriving = coming = None
    own = sources
    for number in range(max(len(source_steps) - 1, len(target_steps))):
        if number < len(target_steps):
            if number:
                targets = jnp.concatenate([targets, arriving], axis=1)
            axis, pairs = target_steps[number]
            arriving = lax.ppermute(targets, axis, pairs)
        if number < len(source_steps) - 1:
            if number:
                sources = jnp.concatenate([sources, coming], axis=1)
            axis, pairs = source_steps[number]
            coming = lax.ppermute(sources, axis, pairs)
    half = targets.shape[1]
    seen = 2 * half
    vmem = (8 << 20) + 4 * (4 * 3 * seen * LANES)
    shapes = [
        ((3, seen, LANES), real),
        ((3, seen, LANES), real),
        ((aggregates, seen), jnp.bfloat16),
    ]

    def scaled(width):
        return pltpu.VMEM((2 * SUBLANES, width), real)

    filled = call(
        functools.partial(first_kernel, True),
        shapes,
        (targets, own, owner),
        pairs=half * count,
        scratch=[scaled(count)],
        vmem=vmem,
    )
    if coming is not None:
        *filled, coming = lax.optimization_barrier((*filled, coming))
        sources = jnp.concatenate([sources, coming], axis=1)
    axis, pairs = source_steps[-1]
    coming = lax.ppermute(sources, axis, pairs)
    filled = call(
        functools.partial(first_kernel, False),
        shapes,
        (targets, own, owner, *filled),
        pairs=half * count,
        scratch=[scaled(count)],
        vmem=vmem,
        aliases={3: 0, 4: 1, 5: 2},
    )
    *filled, arriving = lax.optimization_barrier((*filled, arriving))
    points, total, match = call(
        functools.partial(middle_kernel, count),
        shapes,
        (arriving, sources, owner, *filled),
        pairs=seen * sources.shape[1] - half * count,
        scratch=[scaled(sources.shape[1])],
        vmem=vmem,
        aliases={3: 0, 4: 1, 5: 2},
    )
    targets = jnp.concatenate([targets, arriving], axis=1)
    total, coming = lax.optimization_barrier((total, coming))
    first_row, units = sum_rows(aggregates), seen // count
    unit_rows = velocity_rows(count)
    packed = ((first_row + units // 2 * unit_rows, LANES), real)
    keep, send = call(
        functools.partial(last_kernel, count),
        [packed, packed],
        (points, coming, total, match, targets),
        pairs=seen * coming.shape[1],
        scratch=[
            pltpu.VMEM((3, seen + LANES, LANES), real),
            scaled(sources.shape[1]),
            pltpu.VMEM((seen // LANES + 1, SUBLANES, LANES), real),
        ],
        vmem=vmem,
    )

    for axis, pairs in reversed(target_steps):
        if keep is None:
            half = (both.shape[0] - first_row) // 2
            keep = both[: first_row + half]
            send = jnp.concatenate([both[:first_row], both[first_row + half :]], axis=0)
        both = keep + lax.ppermute(send, axis, pairs)
        keep = None
    sums, mine = both[:first_row], both[first_row:]
    for number, (axis, pairs) in enumerate(source_steps):
        coming = lax.ppermute(sums, axis, pairs)
        if number == 0:
            (velocity,) = call(velocity_kernel, [((3, count), real)], (mine,))
            velocity, coming = lax.optimization_barrier((velocity, coming))
        sums = sums + coming
    columns = aggregates // devices
    (rigid,) = call(rigid_kernel, [((columns, 9), real)], (sums,))
    return velocity, rigid.T


def solution(mesh):
    placed = (
        P(None, ("groups",) + AXES),
        P(None, ("groups",) + AXES),
        P(("groups",) + AXES),
        P("groups"),
    )
    devices = math.prod(mesh.shape[axis] for axis in AXES)
    return jax.shard_map(
        functools.partial(
            on_device, doubling(mesh, SOURCE_AXES), doubling(mesh, TARGET_AXES), devices
        ),
        mesh=mesh,
        in_specs=placed,
        out_specs=(P(None, ("groups",) + AXES), P(None, ("groups",) + AXES)),
        check_vma=False,
    )
```

```python
import functools
import math

import jax
import jax.numpy as jnp
from jax import lax
from jax.experimental import pallas as pl
from jax.experimental.pallas import tpu as pltpu
from jax.sharding import PartitionSpec as P

SCALE = math.sqrt(0.75)
ISO = 9.0 / (32.0 * SCALE)
DYAD = 3.0 * ISO
NEAR = 1.0 / ISO
TOUCH_INVERSE = 1.0 / (2.0 * SCALE)
SMALLEST = 1.1754944e-38

LANES = 128
SUBLANES = 8
GROUPS_AT_ONCE = 4
BLOCKS_AT_ONCE = 4
SUM_ROWS = 16
SOURCE_AXES = ("tgt",)
TARGET_AXES = ("sub", "src")
AXES = ("tgt", "src", "sub")


def add_pairs(
    points_ref, source_ref, before_ref, total_ref, scaled, beside=None, shift=0, unrolled=1
):
    count = total_ref.shape[1] - shift
    blocks = source_ref.shape[1] // LANES
    together = math.gcd(blocks, BLOCKS_AT_ONCE)
    scaled[0:3, :] = SCALE * source_ref[0:3, :]
    scaled[3:6, :] = ISO * source_ref[3:6, :]
    scaled[6:9, :] = DYAD * source_ref[3:6, :]

    def add_block(points, base, block, sums):
        lanes = pl.ds(pl.multiple_of(base + block * LANES, LANES), LANES)
        x, y, z, fx, fy, fz, gx, gy, gz = [
            jnp.broadcast_to(scaled[k : k + 1, lanes], (SUBLANES, LANES)) for k in range(9)
        ]
        result = []
        for number, point in enumerate(points):
            dx, dy, dz = point[0] - x, point[1] - y, point[2] - z
            square = dx * dx + dy * dy + dz * dz
            inverse = lax.rsqrt(jnp.maximum(square, SMALLEST))
            held = jnp.minimum(inverse, TOUCH_INVERSE)
            held_sq = held * held
            iso = jnp.maximum(held * (held_sq + 2.0), NEAR - square * inverse)
            along = dx * gx + dy * gy + dz * gz
            dyad = (inverse * (held_sq * (2.0 / 3.0 - held_sq))) * along
            terms = (iso * fx + dyad * dx, iso * fy + dyad * dy, iso * fz + dyad * dz)
            if sums is not None:
                terms = tuple(one + term for one, term in zip(sums[number], terms))
            result.append(terms)
        return tuple(result)

    def tile_step(step, unused):
        first = step * LANES if isinstance(step, int) else pl.multiple_of(step * LANES, LANES)
        if beside is not None:
            beside(first)
        for group in range(0, LANES // SUBLANES, GROUPS_AT_ONCE):
            starts = [(group + one) * SUBLANES for one in range(GROUPS_AT_ONCE)]
            rows = [pl.ds(first + start, SUBLANES) for start in starts]
            points = [[points_ref[k, one, :] for k in range(3)] for one in rows]
            sums = None
            if before_ref is not None:
                sums = tuple(tuple(before_ref[k, one, :] for k in range(3)) for one in rows)
            if blocks == together:
                for block in range(together):
                    sums = add_block(points, 0, block, sums)
            else:

                def source_step(number, sums):
                    for block in range(together):
                        sums = add_block(points, number * (together * LANES), block, sums)
                    return sums

                zero = jnp.zeros((SUBLANES, LANES), jnp.float32)
                sums = lax.fori_loop(
                    0, blocks // together, source_step, sums or ((zero,) * 3,) * GROUPS_AT_ONCE
                )
            for start, one in zip(starts, sums):
                for k in range(3):
                    total_ref[k, pl.ds(first + shift + start, SUBLANES), :] = one[k]
        return unused

    tiles = count // LANES
    if tiles <= unrolled:
        for tile in range(tiles):
            tile_step(tile, 0)
    else:
        lax.fori_loop(0, tiles, tile_step, 0, unroll=2 if tiles % 2 == 0 else 1)


def head_kernel(
    position_in,
    force_in,
    member_in,
    owner_in,
    source_ref,
    target_ref,
    owner_ref,
    position,
    force,
    member,
    arrived,
):
    moves = [(position_in, position), (force_in, force), (member_in, member), (owner_in, owner_ref)]
    copies = [
        pltpu.make_async_copy(there, here, arrived.at[number])
        for number, (there, here) in enumerate(moves)
    ]
    for copy in copies:
        copy.start()
    for copy in copies:
        copy.wait()
    source_ref[0:3, :] = position[...]
    source_ref[3:6, :] = force[...]
    target_ref[0:3, :] = position[...]
    target_ref[3:4, :] = member[...].astype(jnp.float32)


def place_targets(offset, target_ref, owner_ref, points_ref, match_ref):
    count = target_ref.shape[1]
    parts, rest = [], SCALE * target_ref[0:3, :]
    for _ in range(3):
        part = rest.astype(jnp.bfloat16).astype(jnp.float32)
        rest = rest - part
        parts.append(part)
    parts.append(jnp.zeros((7, count), jnp.float32))
    row = lax.broadcasted_iota(jnp.int32, (16, 3 * LANES), 0)
    lane = lax.broadcasted_iota(jnp.int32, (16, 3 * LANES), 1)
    chosen = jnp.where((row % 3 == lane // LANES) & (row < 9), 1.0, 0.0)
    stacked = jnp.concatenate(parts, axis=0).astype(jnp.bfloat16)
    for start in range(0, count, LANES):
        points = lax.dot_general(
            stacked[:, start : start + LANES],
            chosen.astype(jnp.bfloat16),
            (((0,), (0,)), ((), ())),
            preferred_element_type=jnp.float32,
        )
        rows = slice(offset + start, offset + start + LANES)
        for k in range(3):
            points_ref[k, rows, :] = points[:, k * LANES : (k + 1) * LANES]
    aggregates = match_ref.shape[0]
    labels = lax.broadcasted_iota(jnp.int32, (aggregates, count), 0)
    member = jnp.where(labels == target_ref[3:4, :].astype(jnp.int32), 1.0, 0.0)
    columns = lax.broadcasted_iota(jnp.int32, (aggregates, aggregates), 0)
    owner = jnp.where(columns == owner_ref[...], 1.0, 0.0)
    match_ref[:, offset : offset + count] = jnp.dot(
        owner.astype(jnp.bfloat16),
        member.astype(jnp.bfloat16),
        preferred_element_type=jnp.float32,
    ).astype(jnp.bfloat16)


def first_kernel(early, target_ref, source_ref, owner_ref, *refs):
    points_ref, total_ref, match_ref, scaled = refs[-4:]
    near = pl.ds(0, target_ref.shape[1])
    axis = SOURCE_AXES[0]
    first_half = 2 * lax.axis_index(axis) < lax.axis_size(axis)

    @pl.when(first_half if early else jnp.logical_not(first_half))
    def _():
        place_targets(0, target_ref, owner_ref, points_ref, match_ref)
        add_pairs(
            points_ref.at[:, near, :],
            source_ref,
            None,
            total_ref.at[:, near, :],
            scaled,
            unrolled=4,
        )


def middle_kernel(count, target_ref, source_ref, owner_ref, *refs):
    points_ref, total_ref, match_ref, scaled = refs[-4:]
    half, sources = target_ref.shape[1], source_ref.shape[1]
    near, far, rest = pl.ds(0, half), pl.ds(half, half), sources - count
    some = total_ref.at[:, near, :]
    place_targets(half, target_ref, owner_ref, points_ref, match_ref)
    if rest:
        add_pairs(
            points_ref.at[:, near, :],
            source_ref.at[:, pl.ds(count, rest)],
            some,
            some,
            scaled.at[:, pl.ds(0, rest)],
            unrolled=4,
        )
    add_pairs(points_ref.at[:, far, :], source_ref, None, total_ref.at[:, far, :], scaled)


def last_kernel(
    unit_count,
    points_ref,
    source_ref,
    before_ref,
    match_ref,
    target_ref,
    keep_ref,
    send_ref,
    total,
    scaled,
    summed,
):
    count = target_ref.shape[1]
    tiles = count // LANES

    def sum_tile(first, tile):
        rows = pl.ds(first, LANES)
        for k in range(3):
            summed[tile, k : k + 1, :] = jnp.sum(total[k, rows, :].T, axis=0, keepdims=True)

    total[:, 0:LANES, :] = jnp.zeros((3, LANES, LANES), jnp.float32)
    add_pairs(
        points_ref,
        source_ref,
        before_ref,
        total,
        scaled,
        lambda first: sum_tile(first, first // LANES),
        LANES,
    )
    sum_tile(count, tiles)

    aggregates = match_ref.shape[0]
    per_unit, units = unit_count // LANES, count // unit_count
    first_row, unit_rows = sum_rows(aggregates), velocity_rows(unit_count)
    keep_ref[...] = jnp.zeros_like(keep_ref)
    send_ref[...] = jnp.zeros_like(send_ref)
    u = []
    for k in range(3):
        parts = [summed[tile + 1, k : k + 1, :] for tile in range(tiles)]
        u.append(jnp.concatenate(parts, axis=1))
        for tile in range(tiles):
            unit, block = divmod(tile, per_unit)
            packed, unit = (keep_ref, unit) if unit < units // 2 else (send_ref, unit - units // 2)
            row = first_row + unit * unit_rows + k * per_unit + block
            packed[row : row + 1, :] = parts[tile]
    x = [target_ref[k : k + 1, :] for k in range(3)]
    moments = jnp.concatenate(
        u
        + [
            x[1] * u[2] - x[2] * u[1],
            x[2] * u[0] - x[0] * u[2],
            x[0] * u[1] - x[1] * u[0],
        ]
        + x
        + [jnp.ones((1, count), jnp.float32), jnp.zeros((SUM_ROWS - 10, count), jnp.float32)],
        axis=0,
    )
    parts, rest = [], moments
    for _ in range(3):
        part = rest.astype(jnp.bfloat16)
        rest = rest - part.astype(jnp.float32)
        parts.append(part)
    products = [
        lax.dot_general(
            part,
            match_ref[...],
            (((1,), (1,)), ((), ())),
            preferred_element_type=jnp.float32,
        )
        for part in parts
    ]
    sums = (products[2] + products[1]) + products[0]
    for chunk, start in enumerate(range(0, aggregates, LANES)):
        width = min(LANES, aggregates - start)
        for packed in (keep_ref, send_ref):
            packed[chunk * SUM_ROWS : (chunk + 1) * SUM_ROWS, 0:width] = sums[
                :, start : start + width
            ]


def velocity_kernel(packed_ref, out_ref):
    per_unit = out_ref.shape[1] // LANES
    for k in range(3):
        for block in range(per_unit):
            row = k * per_unit + block
            out_ref[k : k + 1, block * LANES : (block + 1) * LANES] = packed_ref[row : row + 1, :]


def rigid_kernel(sums_ref, out_ref):
    columns = out_ref.shape[0]
    first = lax.axis_index(AXES) * columns
    lane = lax.broadcasted_iota(jnp.int32, (SUM_ROWS, LANES), 1)
    for column in range(columns):
        wanted = first + column
        mine = jnp.zeros((SUM_ROWS, LANES), jnp.float32)
        for chunk in range(sums_ref.shape[0] // SUM_ROWS):
            sums = sums_ref[chunk * SUM_ROWS : (chunk + 1) * SUM_ROWS, :]
            mine = jnp.where(lane + chunk * LANES == wanted, sums, mine)
        mine = jnp.where(lane == wanted % LANES, mine, 0.0)
        mine = jnp.sum(mine, axis=1, keepdims=True)
        u = [mine[k : k + 1] for k in range(3)]
        moment = [mine[3 + k : 4 + k] for k in range(3)]
        centre = [mine[6 + k : 7 + k] / mine[9:10] for k in range(3)]
        torque = [
            moment[0] - (centre[1] * u[2] - centre[2] * u[1]),
            moment[1] - (centre[2] * u[0] - centre[0] * u[2]),
            moment[2] - (centre[0] * u[1] - centre[1] * u[0]),
        ]
        for row, value in enumerate(u + torque + centre):
            out_ref[column : column + 1, row : row + 1] = value


def sum_rows(aggregates):
    return SUM_ROWS * pl.cdiv(aggregates, LANES)


def velocity_rows(count):
    return SUBLANES * pl.cdiv(3 * (count // LANES), SUBLANES)


WHOLE = pl.BlockSpec(memory_space=pltpu.VMEM)


def call(
    kernel, shapes, arguments, pairs=0, scratch=(), specs=None, vmem=8 << 20, aliases={}
):
    return pl.pallas_call(
        kernel,
        out_shape=[jax.ShapeDtypeStruct(shape, dtype) for shape, dtype in shapes],
        in_specs=specs or [WHOLE] * len(arguments),
        out_specs=[WHOLE] * len(shapes),
        scratch_shapes=list(scratch),
        input_output_aliases=aliases,
        compiler_params=pltpu.CompilerParams(vmem_limit_bytes=vmem),
        cost_estimate=pl.CostEstimate(
            flops=40 * pairs + 1000, bytes_accessed=1000, transcendentals=pairs
        ),
    )(*arguments)


def doubling(mesh, axes):
    steps = []
    cores = mesh.shape["sub"]
    other = 1 if cores == 2 else 0
    for axis in axes:
        size = mesh.shape[axis]
        reach = 1
        while reach < size:
            if axis == "sub":
                steps.append((axis, [(i, i ^ reach) for i in range(size)]))
            else:
                flip = reach * cores + other
                steps.append(((axis, "sub"), [(i, i ^ flip) for i in range(size * cores)]))
            reach *= 2
    return steps


def on_device(source_steps, target_steps, devices, positions, forces, membership, owner_slot):
    count, aggregates = positions.shape[1], owner_slot.shape[0]
    real = jnp.float32
    sources, targets, owner = call(
        head_kernel,
        [((6, count), real), ((4, count), real), ((1, aggregates), jnp.int32)],
        [
            pltpu.with_memory_space_constraint(one, pltpu.HBM)
            for one in (positions, forces, membership[None, :], owner_slot[None, :])
        ],
        scratch=[
            pltpu.VMEM((3, count), real),
            pltpu.VMEM((3, count), real),
            pltpu.VMEM((1, count), jnp.int32),
            pltpu.SemaphoreType.DMA((4,)),
        ],
        specs=[pl.BlockSpec(memory_space=pltpu.HBM)] * 4,
    )

    arriving = coming = None
    own = sources
    for number in range(max(len(source_steps) - 1, len(target_steps))):
        if number < len(target_steps):
            if number:
                targets = jnp.concatenate([targets, arriving], axis=1)
            axis, pairs = target_steps[number]
            arriving = lax.ppermute(targets, axis, pairs)
        if number < len(source_steps) - 1:
            if number:
                sources = jnp.concatenate([sources, coming], axis=1)
            axis, pairs = source_steps[number]
            coming = lax.ppermute(sources, axis, pairs)
    half = targets.shape[1]
    seen = 2 * half
    vmem = (8 << 20) + 4 * (4 * 3 * seen * LANES)
    shapes = [
        ((3, seen, LANES), real),
        ((3, seen, LANES), real),
        ((aggregates, seen), jnp.bfloat16),
    ]

    def scaled(width):
        return pltpu.VMEM((2 * SUBLANES, width), real)

    filled = call(
        functools.partial(first_kernel, True),
        shapes,
        (targets, own, owner),
        pairs=half * count,
        scratch=[scaled(count)],
        vmem=vmem,
    )
    if coming is not None:
        *filled, coming = lax.optimization_barrier((*filled, coming))
        sources = jnp.concatenate([sources, coming], axis=1)
    axis, pairs = source_steps[-1]
    coming = lax.ppermute(sources, axis, pairs)
    filled = call(
        functools.partial(first_kernel, False),
        shapes,
        (targets, own, owner, *filled),
        pairs=half * count,
        scratch=[scaled(count)],
        vmem=vmem,
        aliases={3: 0, 4: 1, 5: 2},
    )
    *filled, arriving = lax.optimization_barrier((*filled, arriving))
    points, total, match = call(
        functools.partial(middle_kernel, count),
        shapes,
        (arriving, sources, owner, *filled),
        pairs=seen * sources.shape[1] - half * count,
        scratch=[scaled(sources.shape[1])],
        vmem=vmem,
        aliases={3: 0, 4: 1, 5: 2},
    )
    targets = jnp.concatenate([targets, arriving], axis=1)
    total, coming = lax.optimization_barrier((total, coming))
    first_row, units = sum_rows(aggregates), seen // count
    unit_rows = velocity_rows(count)
    packed = ((first_row + units // 2 * unit_rows, LANES), real)
    keep, send = call(
        functools.partial(last_kernel, count),
        [packed, packed],
        (points, coming, total, match, targets),
        pairs=seen * coming.shape[1],
        scratch=[
            pltpu.VMEM((3, seen + LANES, LANES), real),
            scaled(sources.shape[1]),
            pltpu.VMEM((seen // LANES + 1, SUBLANES, LANES), real),
        ],
        vmem=vmem,
    )

    for axis, pairs in reversed(target_steps):
        if keep is None:
            half = (both.shape[0] - first_row) // 2
            keep = both[: first_row + half]
            send = jnp.concatenate([both[:first_row], both[first_row + half :]], axis=0)
        both = keep + lax.ppermute(send, axis, pairs)
        keep = None
    sums, mine = both[:first_row], both[first_row:]
    for number, (axis, pairs) in enumerate(source_steps):
        coming = lax.ppermute(sums, axis, pairs)
        if number == 0:
            (velocity,) = call(velocity_kernel, [((3, count), real)], (mine,))
            velocity, coming = lax.optimization_barrier((velocity, coming))
        sums = sums + coming
    columns = aggregates // devices
    (rigid,) = call(rigid_kernel, [((columns, 9), real)], (sums,))
    return velocity, rigid.T


def solution(mesh):
    placed = (
        P(None, ("groups",) + AXES),
        P(None, ("groups",) + AXES),
        P(("groups",) + AXES),
        P("groups"),
    )
    devices = math.prod(mesh.shape[axis] for axis in AXES)
    return jax.shard_map(
        functools.partial(
            on_device, doubling(mesh, SOURCE_AXES), doubling(mesh, TARGET_AXES), devices
        ),
        mesh=mesh,
        in_specs=placed,
        out_specs=(P(None, ("groups",) + AXES), P(None, ("groups",) + AXES)),
        check_vma=False,
    )
```
